32 devices in a mesh: grp: 4 (over y, x), gx: 8 (over z, core).
Axes of the slice: x: 2, y: 2, z: 4, core: 2. Of those that a mesh axis runs over, the one named last changes fastest.
Arguments:
- velocity: float32 [3, 64, 64, 4096], P(None, 'grp', 'gx'), may hold values from -6 to 6
- noise: float32 [3, 8, 64, 4096], P(None, None, None, 'gx'), may hold values from -6 to 6
- previous: float32 [3, 64, 4096], P(None, None, 'gx'), may hold values from -6 to 6
- decay: float32 [3, 64], replicated, may hold values from 0.6 to 0.99
- stress_factor: float32 [6, 64], replicated, may hold values from 0.2 to 1
- mean_profile: float32 [64], replicated, may hold values from 0.5 to 1.5
Outputs:
- advanced_velocity: float32 [3, 64, 64, 4096], P(None, 'grp', 'gx')
The draws below stay inside these ranges and needn't reach their ends.
All inputs are finite; a program needn't handle non-finite values.
Results may differ from the reference program's by a relative error of at most 0.0003.
Values sent between devices are 32-bit elements; how exact they have to be, the bound alone decides.
No kernel may reach another device: no remote copies, remote signals or barrier semaphores. Data moves between devices by JAX's collectives and lax.ppermute only.
A program may use at most 128 MiB of HBM per device.

```python
import math
import jax
import jax.numpy as jnp

HALF = 32
PL = 8
NY = 4096
NX = 64
NZ = 64


def draw_noise(key, part):
    keys = jax.random.split(key, 5)
    shape = (3, PL, NZ, NY)
    base = jax.random.normal(keys[0], shape, jnp.float32)
    amp_span = jax.random.uniform(keys[1], (3, 1, 1, 1), jnp.float32, 1.5, 2.5)
    amp_wall = jax.random.uniform(keys[2], (3, 1, 1, 1), jnp.float32, 1.5, 2.5)
    phase_span = jax.random.uniform(keys[3], (3, 1, 1, 1), jnp.float32, 0.0, 2.0 * math.pi)
    phase_wall = jax.random.uniform(keys[4], (3, 1, 1, 1), jnp.float32, 0.0, 2.0 * math.pi)
    z_index = jnp.arange(NZ)
    y_index = jnp.arange(NY)
    z_pos = z_index.astype(jnp.float32)[None, None, :, None]
    y_pos = y_index.astype(jnp.float32)[None, None, None, :]
    z_sign = (1 - 2 * (z_index % 2)).astype(jnp.float32)[None, None, :, None]
    y_sign = (1 - 2 * (y_index % 2)).astype(jnp.float32)[None, None, None, :]
    smooth_z = amp_span * (1.0 + 0.4 * jnp.cos(2.0 * math.pi * z_pos / NZ + phase_span))
    smooth_y = amp_wall * (1.0 + 0.4 * jnp.cos(2.0 * math.pi * y_pos / NY + phase_wall))
    total = base + y_sign * smooth_z + z_sign * smooth_y
    return jnp.clip(total, -6.0, 6.0).astype(jnp.float32)


def steps_of(own_key, extent, cuts, smallest, high):
    factor_of, own = 1.0, jax.random.fold_in(own_key, 6)
    for dim, shards_of in cuts:
        draws = jnp.exp(jax.random.uniform(jax.random.fold_in(own, dim), (shards_of,), jnp.float32, smallest / len(cuts), high / len(cuts)))
        factor_of = factor_of * jnp.repeat(draws, extent[dim] // shards_of).reshape([-1 if axis == dim else 1 for axis in range(len(extent))])
    return factor_of


def scatter_about(stream_key, shape, scale, bound, cuts=(), kind=jnp.bfloat16):
    level = steps_of(stream_key, shape, cuts, -0.22, 0.18) if cuts else 1.0
    values = jax.random.normal(stream_key, shape, jnp.float32) * scale * level
    return jnp.minimum(jnp.maximum(values, -bound), bound).astype(kind)


def setup_inputs(seed: int = 0) -> dict:
    arg_keys = jax.random.split(jax.random.key(seed), 7)
    velocity = scatter_about(arg_keys[0], (3, NX, NZ, NY), 1.0, 6.0, ((1, 4), (2, 8)), jnp.float32)
    noise = draw_noise(jax.random.fold_in(arg_keys[6], 71), 0)
    previous = scatter_about(arg_keys[2], (3, NZ, NY), 1.0, 6.0, ((2, 8),), jnp.float32)
    decay = jnp.clip(jnp.exp(jax.random.uniform(arg_keys[3], (3, NZ), jnp.float32, math.log(0.6), math.log(0.99))), 0.6, 0.99)
    stress_factor = jnp.clip(jax.random.uniform(arg_keys[4], (6, NZ), jnp.float32, 0.2, 1.0), 0.2, 1.0)
    mean_profile = jnp.clip(jax.random.uniform(arg_keys[5], (NZ,), jnp.float32, 0.5, 1.5), 0.5, 1.5)
    return {"velocity": velocity, "noise": noise, "previous": previous, "decay": decay, "stress_factor": stress_factor, "mean_profile": mean_profile}


TIME_STEP = 0.15
VISCOSITY = 0.2

def kernel_weight(offset):
    length = HALF / 2.0
    return jnp.exp(-jnp.pi * offset * offset / (2.0 * length * length))

def kernel_norm():
    offsets = jnp.arange(-HALF, HALF + 1).astype(jnp.float32)
    return jnp.sqrt(jnp.sum(kernel_weight(offsets) ** 2))

def smooth(noise):
    norm = kernel_norm()
    along_y = jnp.zeros_like(noise)
    for offset in range(-HALF, HALF + 1):
        weight = kernel_weight(jnp.float32(offset)) / norm
        along_y = along_y + weight * jnp.roll(noise, -offset, axis=3)
    padded = jnp.pad(along_y, ((0, 0), (0, 0), (HALF, HALF), (0, 0)))
    result = jnp.zeros_like(noise)
    for offset in range(-HALF, HALF + 1):
        weight = kernel_weight(jnp.float32(offset)) / norm
        result = result + weight * padded[:, :, HALF + offset:HALF + offset + NZ]
    return result

def colour(planes, stress_factor, mean_profile):
    factor = stress_factor[:, None, :, None]
    first = mean_profile[None, :, None] + factor[0] * planes[0]
    second = factor[1] * planes[0] + factor[2] * planes[1]
    third = factor[3] * planes[0] + factor[4] * planes[1] + factor[5] * planes[2]
    return jnp.stack([first, second, third])

def tendency(padded):
    centre = padded[:, 1:-1, 1:-1]
    x_next = padded[:, 2:, 1:-1]
    x_prev = padded[:, :-2, 1:-1]
    z_next = padded[:, 1:-1, 2:]
    z_prev = padded[:, 1:-1, :-2]
    y_next = jnp.roll(centre, -1, axis=3)
    y_prev = jnp.roll(centre, 1, axis=3)
    advect = centre[0:1] * (x_next - x_prev) * 0.5
    advect = advect + centre[1:2] * (z_next - z_prev) * 0.5
    advect = advect + centre[2:3] * (y_next - y_prev) * 0.5
    spread = x_next + x_prev + z_next + z_prev + y_next + y_prev - 6.0 * centre
    return -advect + VISCOSITY * spread

def pad_faces(field):
    return jnp.pad(field, ((0, 0), (1, 1), (1, 1), (0, 0)))

def reference(velocity, noise, previous, decay, stress_factor, mean_profile):
    smoothed = smooth(noise)
    decay_col = decay[:, :, None]
    scale_col = jnp.sqrt(1.0 - decay_col * decay_col)
    carried = previous
    outputs = []
    for plane_index in range(PL):
        carried = decay_col * carried + scale_col * smoothed[:, plane_index]
        outputs.append(carried)
    planes = jnp.stack(outputs, axis=1)
    inflow = colour(planes, stress_factor, mean_profile)
    start = velocity.at[:, :PL].set(inflow)
    section = start + TIME_STEP * tendency(pad_faces(start))
    second = section + TIME_STEP * tendency(pad_faces(section))
    return 0.5 * start + 0.5 * second
```

```python
import functools
import math

import jax
import jax.numpy as jnp
from jax import lax
from jax.experimental import pallas as pl
from jax.experimental.pallas import tpu as pltpu
from jax.sharding import PartitionSpec as P

HALF = 32
TIME_STEP = 0.15
VISCOSITY = 0.2
LANES = 128
SUB = 8
PARTS = 4
VMEM_LIMIT = 60 * 1024 * 1024

ANY = pl.BlockSpec(memory_space=pl.ANY)
SMEM = pl.BlockSpec(memory_space=pltpu.SMEM)
VMEM = pl.BlockSpec(memory_space=pltpu.VMEM)
F32 = jnp.float32


def params():
    return pltpu.CompilerParams(vmem_limit_bytes=VMEM_LIMIT)


def cost(flops, nbytes):
    return pl.CostEstimate(flops=flops, bytes_accessed=nbytes, transcendentals=0)


def kernel_norm():
    length = HALF / 2.0
    total = sum(
        math.exp(-math.pi * k * k / (2.0 * length * length)) ** 2 for k in range(-HALF, HALF + 1)
    )
    return math.sqrt(total)


def weights(offset):
    length = HALF / 2.0
    off = offset.astype(F32)
    value = jnp.exp(off * off * (-math.pi / (2.0 * length * length))) * (1.0 / kernel_norm())
    return jnp.where(jnp.abs(offset) <= HALF, value, 0.0)


def split(x):
    high = x.astype(jnp.bfloat16)
    low = (x - high.astype(F32)).astype(jnp.bfloat16)
    return high, low


def dot(a, b):
    return jnp.dot(a, b, preferred_element_type=F32)


def rim_kernel(left_ref, noise_ref, out_ref):
    depth = noise_ref.shape[2]
    span = noise_ref.shape[3]
    groups = LANES // HALF
    rows = depth // groups
    lane = lax.broadcasted_iota(jnp.int32, (rows, LANES), 1)
    use_left = left_ref[0] == 1

    def plane(i, _):
        c, p = i // noise_ref.shape[1], i % noise_ref.shape[1]
        result = None
        for q in range(groups):
            first = noise_ref[c, p, rows * q : rows * (q + 1), 0:LANES]
            last = noise_ref[c, p, rows * q : rows * (q + 1), span - LANES : span]
            last = pltpu.roll(last, HALF, 1)
            piece = jnp.where(use_left, first, last)
            if q:
                piece = pltpu.roll(piece, HALF * q, 1)
            result = piece if q == 0 else jnp.where(lane >= HALF * q, piece, result)
        out_ref[c, p] = result
        return 0

    lax.fori_loop(0, noise_ref.shape[0] * noise_ref.shape[1], plane, 0)


def filter_kernel(width, with_rim, meta_ref, noise_ref, rim_ref, prev_ref, decay_ref, factor_ref,
                  mean_ref, out_ref, planes_ref):
    comps, count, depth, span = noise_ref.shape
    base = meta_ref[0]
    rim_at = meta_ref[1]
    row = lax.broadcasted_iota(jnp.int32, (span, width), 0)
    col = lax.broadcasted_iota(jnp.int32, (span, width), 1)
    band_h, band_l = split(weights(row - col - base))
    zrow = lax.broadcasted_iota(jnp.int32, (depth, depth), 0)
    zcol = lax.broadcasted_iota(jnp.int32, (depth, depth), 1)
    zh, zl = split(weights(zrow - zcol))
    zband = jnp.concatenate([zh, zh, zl], axis=1)
    groups = LANES // HALF
    rows = depth // groups
    if with_rim:
        hrow = lax.broadcasted_iota(jnp.int32, (LANES, width), 0)
        hcol = lax.broadcasted_iota(jnp.int32, (LANES, width), 1)
        rim_bands = []
        for q in range(groups):
            cell = hrow - HALF * q
            value = weights(cell + rim_at - hcol - base)
            rim_bands.append(split(jnp.where((cell >= 0) & (cell < HALF), value, 0.0)))
    for c in range(comps):
        high, low = split(noise_ref[c].reshape(count * depth, span))
        along = dot(high, band_h) + dot(low, band_h) + dot(high, band_l)
        along = along.reshape(count, depth, width)
        if with_rim:
            rh, rl = split(rim_ref[c].reshape(count * rows, LANES))
            extra = []
            for bh, bl in rim_bands:
                part = dot(rh, bh) + dot(rl, bh) + dot(rh, bl)
                extra.append(part.reshape(count, rows, width))
            along = along + jnp.concatenate(extra, axis=1)
        wide = jnp.concatenate([along[p] for p in range(count)], axis=1)
        yh, yl = split(wide)
        smooth = dot(zband, jnp.concatenate([yh, yl, yh], axis=0))
        dec = decay_ref[c]
        scale = jnp.sqrt(1.0 - dec * dec)
        carried = prev_ref[c]
        for p in range(count):
            carried = dec * carried + scale * smooth[:, p * width : (p + 1) * width]
            planes_ref[c, p] = carried
    owners = out_ref.shape[0]
    slab = depth // owners

    def put(c, p, value):
        for d in range(owners):
            out_ref[d, c, p] = value[slab * d : slab * (d + 1)]

    for p in range(count):
        a, b, d = planes_ref[0, p], planes_ref[1, p], planes_ref[2, p]
        put(0, p, mean_ref[...] + factor_ref[0] * a)
        put(1, p, factor_ref[1] * a + factor_ref[2] * b)
        put(2, p, factor_ref[3] * a + factor_ref[4] * b + factor_ref[5] * d)


def faces_kernel(vel, low_dn, low_up, high_dn, high_up, tiles, sem):
    blocks = tiles.shape[0]
    copies = [
        pltpu.make_async_copy(vel.at[:, :, pl.ds(t * LANES, LANES)], tiles.at[t], sem.at[t])
        for t in range(blocks)
    ]
    for copy in copies:
        copy.start()
    for copy in copies:
        copy.wait()
    slab = SUB

    def block(t, _):
        at = pl.multiple_of(t * LANES, LANES)
        for c in range(3):
            for dn, up, first in ((low_dn, low_up, 0), (high_dn, high_up, low_dn.shape[2])):
                for j in range(2):
                    for ref, z in ((dn, j), (up, slab - 2 + j)):
                        for x in range(0, dn.shape[2], SUB):
                            ref[c, j, x : x + SUB, pl.ds(at, LANES)] = tiles[
                                t, c, pl.ds((first + x) * slab + z, SUB, stride=slab), :
                            ]
        return 0

    lax.fori_loop(0, blocks, block, 0)


def inflow_faces_kernel(*refs):
    parts = refs[:-2]
    dn, up = refs[-2:]
    width = parts[0].shape[3]
    slab = SUB
    cells = dn.shape[2]
    for k, part in enumerate(parts):
        for s in range(part.shape[0]):
            at = (s * len(parts) + k) * width
            for c in range(part.shape[1]):
                for j in range(2):
                    for ref, z in ((dn, j), (up, slab - 2 + j)):
                        for x in range(0, cells, SUB):
                            ref[c, j, x : x + SUB, at : at + width] = part[
                                s, c, pl.ds(x * slab + z, SUB, stride=slab), :
                            ]


A = VISCOSITY * TIME_STEP
H = 0.5 * TIME_STEP
B = 1.0 - 6.0 * A
BLOCK = 512


def combine(scale, cs, xp, xn, zp, zn, yp, yn):
    a, h, b = A * scale, H * scale, B * scale
    cu, cw, cv = h * cs[0], h * cs[1], h * cs[2]
    out = []
    for i in range(3):
        total = xn[i] * (a - cu) + xp[i] * (a + cu)
        total = total + (zn[i] * (a - cw) + zp[i] * (a + cw))
        total = total + (yn[i] * (a - cv) + yp[i] * (a + cv))
        out.append(total + b * cs[i])
    return out


def spanwise(load, at, width, span):
    centre = load(at, width)
    wide = jnp.concatenate(
        [load((at - LANES) % span, LANES), centre, load((at + width) % span, LANES)], axis=1
    )
    total = width + 2 * LANES
    before = pltpu.roll(wide, 1, 1)[:, LANES : LANES + width]
    after = pltpu.roll(wide, total - 1, 1)[:, LANES : LANES + width]
    return centre, before, after


def main_block(scale, field, x, zb, za, zrow, at, width, span):
    top = lax.broadcasted_iota(jnp.int32, (SUB, width), 0)
    cs, xp, xn, zp, zn, yp, yn = [], [], [], [], [], [], []
    for c in range(3):
        centre, before, after = spanwise(
            lambda l, w, c=c: field[c, x, :, pl.ds(l, w)], at, width, span
        )
        cs.append(centre)
        yp.append(before)
        yn.append(after)
        xp.append(field[c, x - 1, :, pl.ds(at, width)])
        xn.append(field[c, x + 1, :, pl.ds(at, width)])
        low = jnp.broadcast_to(zb[c, pl.ds(zrow, 1), pl.ds(at, width)], (SUB, width))
        high = jnp.broadcast_to(za[c, pl.ds(zrow, 1), pl.ds(at, width)], (SUB, width))
        zp.append(jnp.where(top == 0, low, pltpu.roll(centre, 1, 0)))
        zn.append(jnp.where(top == SUB - 1, high, pltpu.roll(centre, SUB - 1, 0)))
    return combine(scale, cs, xp, xn, zp, zn, yp, yn)


def edge_rows(near, before, after, out, keep, groups, span):
    def block(i, _):
        at = pl.multiple_of(i * BLOCK, BLOCK)
        left = pl.multiple_of(lax.rem(at + span - LANES, span), LANES)
        right = pl.multiple_of(lax.rem(at + BLOCK, span), LANES)
        for g in range(groups):
            cs, xp, xn, zp, zn, yp, yn = [], [], [], [], [], [], []
            for c in range(3):
                r = SUB * (g + 1)
                centre = near[c, r : r + SUB, pl.ds(at, BLOCK)]
                wide = jnp.concatenate(
                    [
                        near[c, r : r + SUB, pl.ds(left, LANES)],
                        centre,
                        near[c, r : r + SUB, pl.ds(right, LANES)],
                    ],
                    axis=1,
                )
                total = BLOCK + 2 * LANES
                cs.append(centre)
                yp.append(pltpu.roll(wide, 1, 1)[:, LANES : LANES + BLOCK])
                yn.append(pltpu.roll(wide, total - 1, 1)[:, LANES : LANES + BLOCK])
                xp.append(near[c, r - 1 : r - 1 + SUB, pl.ds(at, BLOCK)])
                xn.append(near[c, r + 1 : r + 1 + SUB, pl.ds(at, BLOCK)])
                zp.append(before[c, SUB * g : SUB * (g + 1), pl.ds(at, BLOCK)])
                zn.append(after[c, SUB * g : SUB * (g + 1), pl.ds(at, BLOCK)])
            new = combine(1.0, cs, xp, xn, zp, zn, yp, yn)
            for c in range(3):
                out[c, SUB * (g + 1) : SUB * (g + 2), pl.ds(at, BLOCK)] = jnp.where(
                    keep, new[c], 0.0
                )
        return 0

    lax.fori_loop(0, span // BLOCK, block, 0)


def section_plane(x, start, sect, nb, na, span, keep=None):
    for at in range(0, span, BLOCK):
        new = main_block(1.0, start, x + 2, nb, na, SUB + x, at, BLOCK, span)
        for c in range(3):
            value = new[c] if keep is None else jnp.where(keep, new[c], 0.0)
            sect[c, x + 1, :, at : at + BLOCK] = value


def second_plane(x, start, sect, eb, ea, out, span):
    for at in range(0, span, BLOCK):
        new = main_block(0.5, sect, x + 1, eb, ea, SUB + x, at, BLOCK, span)
        for c in range(3):
            out[c, x, :, at : at + BLOCK] = new[c] + 0.5 * start[c, x + 2, :, at : at + BLOCK]


def rows_scratch(cells, span):
    shift = [
        pltpu.VMEM((3, cells + 2 * SUB, span), F32),
        pltpu.VMEM((3, cells + 2 * SUB, span), F32),
    ]
    side = [pltpu.VMEM((3, cells, span), F32)] * 4
    return shift + side + shift


def run_copies(copies):
    for copy in copies:
        copy.start()
    for copy in copies:
        copy.wait()


def own_kernel(meta, vel, left, right, corners, dn_lo, dn_hi, up_lo, up_hi, b_lo, b_hi, a_lo, a_hi,
               out_hbm, start, sect, out, nb, na, b2, b0, a0, a2, eb, ea, corner, sem, out_sem):
    cells = vel.shape[1]
    low = dn_lo.shape[2]
    span = vel.shape[3]
    pieces = [
        (vel, start.at[:, pl.ds(2, cells)]),
        (left, start.at[:, pl.ds(0, 2)]),
        (right, start.at[:, pl.ds(cells + 2, 2)]),
        (corners, corner),
    ]
    for lo, hi, j, ref, first in (
        (b_lo, b_hi, 1, nb, SUB),
        (a_lo, a_hi, 0, na, SUB),
        (b_lo, b_hi, 0, b2, 0),
        (a_lo, a_hi, 1, a2, 0),
        (dn_lo, dn_hi, 0, b0, 0),
        (up_lo, up_hi, 1, a0, 0),
    ):
        pieces.append((lo.at[:, j], ref.at[:, pl.ds(first, low)]))
        pieces.append((hi.at[:, j], ref.at[:, pl.ds(first + low, cells - low)]))
    run_copies(
        [pltpu.make_async_copy(src, dst, sem.at[i]) for i, (src, dst) in enumerate(pieces)]
    )
    for c in range(3):
        nb[c, SUB - 1 : SUB, :] = corner[c, 0:1, :]
        nb[c, SUB + cells : SUB + cells + 1, :] = corner[c, 1:2, :]
        na[c, SUB - 1 : SUB, :] = corner[c, 2:3, :]
        na[c, SUB + cells : SUB + cells + 1, :] = corner[c, 3:4, :]
    groups = cells // SUB
    edge_rows(nb, b2, b0, eb, meta[0] == 1, groups, span)
    edge_rows(na, a0, a2, ea, meta[1] == 1, groups, span)
    first = meta[4]

    def make(x, keep=None):
        section_plane(x, start, sect, nb, na, span, keep)

    def body(x, _):
        keep = jnp.logical_or(
            jnp.logical_and(x >= 0, x < cells),
            jnp.where(x < 0, meta[2], meta[3]) == 1,
        )
        make(x, keep)

        @pl.when(x >= first + 1)
        def _():
            second_plane(x - 1, start, sect, eb, ea, out, span)
            pltpu.make_async_copy(out.at[:, x - 1], out_hbm.at[:, x - 1], out_sem.at[x - 1]).start()

        return 0

    lax.fori_loop(first - 1, cells + 1, body, 0)

    def drain(x, _):
        pltpu.make_async_copy(out.at[:, x], out_hbm.at[:, x], out_sem.at[x]).wait()
        return 0

    lax.fori_loop(first, cells, drain, 0)


def inflow_kernel(meta, vel, *refs):
    parts, refs = refs[:-23], refs[-23:]
    dn_in, up_in, b_in, a_in, dn_hi, up_hi, b_hi, a_hi, _, out_hbm = refs[:10]
    start, sect, out, nb, na, b2, b0, a0, a2, eb, ea, sem, out_sem = refs[10:]
    low = dn_in.shape[2]
    span = vel.shape[3]
    reach = out.shape[1]
    cells = b2.shape[1]

    @pl.when(meta[5] == 1)
    def _():
        pieces = [(vel.at[:, pl.ds(low, 4)], start.at[:, pl.ds(low + 2, 4)])]
        width = parts[0].shape[4]
        for k, part in enumerate(parts):
            for s in range(part.shape[0]):
                at = (s * len(parts) + k) * width
                pieces.append((part.at[s], start.at[:, pl.ds(2, low), :, pl.ds(at, width)]))
        for lo, hi, j, ref, first in (
            (b_in, b_hi, 1, nb, SUB),
            (a_in, a_hi, 0, na, SUB),
            (b_in, b_hi, 0, b2, 0),
            (a_in, a_hi, 1, a2, 0),
            (dn_in, dn_hi, 0, b0, 0),
            (up_in, up_hi, 1, a0, 0),
        ):
            pieces.append((lo.at[:, j], ref.at[:, pl.ds(first, low)]))
            pieces.append((hi.at[:, j], ref.at[:, pl.ds(first + low, cells - low)]))
        copies = [
            pltpu.make_async_copy(src, dst, sem.at[i]) for i, (src, dst) in enumerate(pieces)
        ]
        for copy in copies:
            copy.start()
        zero = jnp.zeros((SUB, span), F32)
        for c in range(3):
            start[c, 1] = zero
            sect[c, 0] = zero
            for ref in (nb, na):
                ref[c, 0:SUB, :] = zero
                ref[c, SUB + cells :, :] = zero
        for copy in copies:
            copy.wait()
        groups = cells // SUB
        edge_rows(nb, b2, b0, eb, meta[0] == 1, groups, span)
        edge_rows(na, a0, a2, ea, meta[1] == 1, groups, span)
        section_plane(0, start, sect, nb, na, span)

        def body(x, _):
            section_plane(x + 1, start, sect, nb, na, span)
            second_plane(x, start, sect, eb, ea, out, span)
            pltpu.make_async_copy(out.at[:, x], out_hbm.at[:, x], out_sem.at[x]).start()
            return 0

        lax.fori_loop(0, reach, body, 0)

        def drain(x, _):
            pltpu.make_async_copy(out.at[:, x], out_hbm.at[:, x], out_sem.at[x]).wait()
            return 0

        lax.fori_loop(0, reach, drain, 0)


def shift(array, axis, step, count, wrap=False):
    pairs = [(i, (i + step) % count) for i in range(count) if wrap or 0 <= i + step < count]
    return lax.ppermute(array, axis, pairs)


def on_lines(array, lines, step, count):
    pairs = [
        (r * count + i, r * count + i + step) for r in lines for i in range(count)
        if 0 <= i + step < count
    ]
    return lax.ppermute(array, ("grp", "gx"), pairs)


def local(velocity, noise, previous, decay, stress_factor, mean_profile):
    rows = lax.axis_size("grp")
    ranks = lax.axis_size("gx")
    r = lax.axis_index("grp")
    g = lax.axis_index("gx")
    comps, count, depth, span_local = noise.shape
    cells, slab, span = velocity.shape[1:]
    width = span_local // PARTS
    low = count
    high = cells - low

    packed = (comps, count, depth * HALF // LANES, LANES)
    is_second = (r == 2).astype(jnp.int32)
    rim_out = pl.pallas_call(
        rim_kernel,
        out_shape=jax.ShapeDtypeStruct(packed, F32),
        in_specs=[SMEM, VMEM],
        out_specs=VMEM,
        compiler_params=params(),
        cost_estimate=cost(0, 4 * noise.size),
        name="rim",
    )(is_second.reshape(1), noise)
    pairs = []
    for line in range(rows):
        step = -1 if line == 2 else 1
        pairs += [(line * ranks + i, line * ranks + (i + step) % ranks) for i in range(ranks)]
    rim = lax.ppermute(rim_out, ("grp", "gx"), pairs)

    face = jax.ShapeDtypeStruct((3, 2, low, span), F32)
    face_hi = jax.ShapeDtypeStruct((3, 2, high, span), F32)
    dn_lo, up_lo, dn_hi, up_hi = pl.pallas_call(
        faces_kernel,
        out_shape=[face, face, face_hi, face_hi],
        in_specs=[ANY],
        out_specs=[VMEM] * 4,
        scratch_shapes=[
            pltpu.VMEM((span // LANES, 3, cells * slab, LANES), F32),
            pltpu.SemaphoreType.DMA((span // LANES,)),
        ],
        compiler_params=params(),
        cost_estimate=cost(0, 8 * velocity.size),
        name="faces",
    )(velocity.reshape(3, cells * slab, span))
    b_hi = shift(up_hi, "gx", 1, ranks)
    a_hi = shift(dn_hi, "gx", -1, ranks)
    left = shift(velocity[:, cells - 2 :], "grp", 1, rows)
    right = shift(velocity[:, :2], "grp", -1, rows)
    up_corner = jnp.stack([left[:, 1, slab - 1], right[:, 0, slab - 1]], axis=1)
    dn_corner = jnp.stack([left[:, 1, 0], right[:, 0, 0]], axis=1)
    corners = jnp.concatenate(
        [shift(up_corner, "gx", 1, ranks), shift(dn_corner, "gx", -1, ranks)], axis=1
    )

    wide = (comps, depth, width)
    decay_wide = jnp.broadcast_to(decay[:, :, None], wide)
    factor_wide = jnp.broadcast_to(stress_factor[:, :, None], (6, depth, width))
    mean_wide = jnp.broadcast_to(mean_profile[:, None], (depth, width))

    def make(part, with_rim):
        base = part * width
        meta = jnp.stack([base, jnp.where(r == 2, span_local, -HALF)]).astype(jnp.int32)
        prev = lax.dynamic_slice_in_dim(previous, base, width, 2)
        return pl.pallas_call(
            functools.partial(filter_kernel, width, with_rim),
            out_shape=jax.ShapeDtypeStruct((ranks, comps, count, depth // ranks, width), F32),
            in_specs=[SMEM] + [VMEM] * 6,
            out_specs=VMEM,
            scratch_shapes=[pltpu.VMEM((comps, count, depth, width), F32)],
            compiler_params=params(),
            cost_estimate=cost(6 * noise.size * width, 4 * noise.size),
            name="filter_a" if with_rim else "filter_b",
        )(meta, noise, rim if with_rim else rim_out, prev, decay_wide, factor_wide, mean_wide)

    part_a = jnp.where(r == 1, 0, jnp.where(r == 2, 3, 1))
    made_a = make(part_a, True)
    made_b = make(jnp.int32(2), False)
    got_a = lax.all_to_all(made_a, "gx", 0, 0, tiled=True)
    got_b = lax.all_to_all(made_b, "gx", 0, 0, tiled=True)
    hop_1 = lax.ppermute(got_a, "grp", [(1, 0)])
    hop_2 = lax.ppermute(got_a, "grp", [(2, 0)])
    parts = [hop_1, got_a, got_b, hop_2]
    if width != LANES:
        joined = jnp.concatenate(parts, axis=4)
        parts = [joined[..., at : at + LANES] for at in range(0, span_local, LANES)]
    many, part_width = len(parts), parts[0].shape[4]

    others = list(range(1, rows))
    b_lo = on_lines(up_lo, others, 1, ranks)
    a_lo = on_lines(dn_lo, others, -1, ranks)

    meta = jnp.stack(
        [
            g > 0,
            g < ranks - 1,
            r > 0,
            r < rows - 1,
            jnp.where(r == 0, low + 2, 0),
            r == 0,
        ]
    ).astype(jnp.int32)

    full = jax.ShapeDtypeStruct(velocity.shape, F32)
    own = pl.pallas_call(
        own_kernel,
        out_shape=full,
        in_specs=[SMEM] + [ANY] * 12,
        out_specs=ANY,
        scratch_shapes=[
            pltpu.VMEM((3, cells + 4, slab, span), F32),
            pltpu.VMEM((3, cells + 2, slab, span), F32),
            pltpu.VMEM((3, cells, slab, span), F32),
        ]
        + rows_scratch(cells, span)
        + [
            pltpu.VMEM((3, 4, span), F32),
            pltpu.SemaphoreType.DMA((16,)),
            pltpu.SemaphoreType.DMA((cells,)),
        ],
        compiler_params=params(),
        cost_estimate=cost(50 * velocity.size, 8 * velocity.size),
        name="own",
    )(meta, velocity, left, right, corners, dn_lo, dn_hi, up_lo, up_hi, b_lo, b_hi, a_lo, a_hi)

    dn_in, up_in = pl.pallas_call(
        inflow_faces_kernel,
        out_shape=[face, face],
        in_specs=[VMEM] * many,
        out_specs=[VMEM] * 2,
        compiler_params=params(),
        cost_estimate=cost(0, 8 * noise.size),
        name="inflow_faces",
    )(*[p.reshape(ranks, comps, count * slab, part_width) for p in parts])
    b_in = on_lines(up_in, [0], 1, ranks)
    a_in = on_lines(dn_in, [0], -1, ranks)

    reach = low + 2
    return pl.pallas_call(
        inflow_kernel,
        out_shape=full,
        in_specs=[SMEM] + [ANY] * (many + 10),
        out_specs=ANY,
        scratch_shapes=[
            pltpu.VMEM((3, reach + 4, slab, span), F32),
            pltpu.VMEM((3, reach + 2, slab, span), F32),
            pltpu.VMEM((3, reach, slab, span), F32),
        ]
        + rows_scratch(low + high, span)
        + [
            pltpu.SemaphoreType.DMA((many * ranks + 13,)),
            pltpu.SemaphoreType.DMA((reach,)),
        ],
        input_output_aliases={many + 10: 0},
        compiler_params=params(),
        cost_estimate=cost(30 * velocity.size, 5 * velocity.size),
        name="inflow",
    )(meta, velocity, *parts, dn_in, up_in, b_in, a_in, dn_hi, up_hi, b_hi, a_hi, own)


def solution(mesh):
    placed = (
        P(None, "grp", "gx", None),
        P(None, None, None, "gx"),
        P(None, None, "gx"),
        P(),
        P(),
        P(),
    )
    return jax.shard_map(
        local, mesh=mesh, in_specs=placed, out_specs=P(None, "grp", "gx", None), check_vma=False
    )
```

```python
import functools
import math

import jax
import jax.numpy as jnp
from jax import lax
from jax.experimental import pallas as pl
from jax.experimental.pallas import tpu as pltpu
from jax.sharding import PartitionSpec as P


HALF = 32
TIME_STEP = 0.15
VISCOSITY = 0.2
LANES = 128
SUB = 8
PARTS = 4
VMEM_LIMIT = 60 * 1024 * 1024

ANY = pl.BlockSpec(memory_space=pltpu.HBM)
VMEM = pl.BlockSpec(memory_space=pltpu.VMEM)
F32 = jnp.float32


def params():
    return pltpu.CompilerParams(vmem_limit_bytes=VMEM_LIMIT)


def cost(flops, nbytes):
    return pl.CostEstimate(flops=flops, bytes_accessed=nbytes, transcendentals=0)


def kernel_norm():
    length = HALF / 2.0
    total = sum(
        math.exp(-math.pi * k * k / (2.0 * length * length)) ** 2 for k in range(-HALF, HALF + 1)
    )
    return math.sqrt(total)


def weights(offset):
    length = HALF / 2.0
    off = offset.astype(F32)
    value = jnp.exp(off * off * (-math.pi / (2.0 * length * length))) * (1.0 / kernel_norm())
    return jnp.where(jnp.abs(offset) <= HALF, value, 0.0)


def split(x):
    high = x.astype(jnp.bfloat16)
    low = (x - high.astype(F32)).astype(jnp.bfloat16)
    return high, low


def dot(a, b):
    return jnp.dot(a, b, preferred_element_type=F32)


def first_kernel(noise, rim_ref, edge, sem):
    comps, count, depth, span = noise.shape
    groups = LANES // HALF
    rows = depth // groups
    use_left = lax.axis_index("grp") == 2
    at = pl.multiple_of(jnp.where(use_left, 0, span - LANES), LANES)
    copies = [
        pltpu.make_async_copy(noise.at[c, :, :, pl.ds(at, LANES)], edge.at[c], sem.at[c])
        for c in range(comps)
    ]
    for copy in copies:
        copy.start()
    lane = lax.broadcasted_iota(jnp.int32, (count, rows, LANES), 2)
    for c in range(comps):
        copies[c].wait()
        result = None
        for q in range(groups):
            piece = edge[c, :, rows * q : rows * (q + 1), :]
            to_left = piece if q == 0 else pltpu.roll(piece, HALF * q, 2)
            to_right = pltpu.roll(piece, (HALF * (q + 1)) % LANES, 2) if (q + 1) % groups else piece
            piece = jnp.where(use_left, to_left, to_right)
            result = piece if q == 0 else jnp.where(lane >= HALF * q, piece, result)
        rim_ref[c] = result


def face_copies(vel, first, cells, dn, up, sem, at):
    slab = vel.shape[2]
    copies = []
    for c in range(3):
        for j in range(2):
            for ref, z in ((dn, j), (up, slab - 2 + j)):
                copies.append(
                    pltpu.make_async_copy(
                        vel.at[c, pl.ds(first, cells), z], ref.at[c, j], sem.at[at + len(copies)]
                    )
                )
    return copies


def xfaces_kernel(vel, after, near_ref, far_ref, sem):
    del after
    cells = vel.shape[1]
    even = lax.rem(lax.axis_index("grp"), 2) == 0
    at = jnp.where(even, cells - 2, 0)
    run_copies(
        [
            pltpu.make_async_copy(vel.at[:, pl.ds(at, 2)], near_ref, sem.at[0]),
            pltpu.make_async_copy(vel.at[:, pl.ds(cells - 2 - at, 2)], far_ref, sem.at[1]),
        ]
    )


def zfaces_kernel(vel, after, all_dn, all_up, high_dn, high_up, sem):
    del after
    cells, high = all_dn.shape[2], high_dn.shape[2]
    is_first = lax.axis_index("grp") == 0

    @pl.when(is_first)
    def _():
        run_copies(face_copies(vel, cells - high, high, high_dn, high_up, sem, 0))

    @pl.when(jnp.logical_not(is_first))
    def _():
        run_copies(face_copies(vel, 0, cells, all_dn, all_up, sem, 0))


def mark_kernel(after, out_ref):
    del after
    out_ref[...] = jnp.zeros_like(out_ref)


def column(ref, c, width):
    depth = ref.shape[1]
    row = lax.broadcasted_iota(jnp.int32, (depth, depth), 0)
    col = lax.broadcasted_iota(jnp.int32, (depth, depth), 1)
    value = jnp.where(row == col, jnp.broadcast_to(ref[c : c + 1, :], (depth, depth)), 0.0)
    return jnp.broadcast_to(jnp.sum(value, axis=1, keepdims=True), (depth, width))


def part_of(line):
    return jnp.where(line == 0, 1, jnp.where(line == 1, 0, jnp.where(line == 2, PARTS - 1, 2)))


def window_of(line, width, whole, span):
    first = part_of(line) * width
    start = jnp.minimum(jnp.maximum((first - HALF) // LANES * LANES, 0), whole - span)
    return first, pl.multiple_of(start, LANES)


def spanwise_band(base, span, width):
    row = lax.broadcasted_iota(jnp.int32, (span, width), 0)
    col = lax.broadcasted_iota(jnp.int32, (span, width), 1)
    high, low = split(weights(row - col - base))
    return jnp.concatenate([high, high, low], axis=0)


def window_copies(noise, noise_ref, start, sem):
    comps, _, _, span = noise_ref.shape
    return [
        pltpu.make_async_copy(noise.at[c, :, :, pl.ds(start, span)], noise_ref.at[c], sem.at[c])
        for c in range(comps)
    ]


def along_kernel(noise, out_ref, noise_ref, sem):
    comps, count, depth, span = noise_ref.shape
    width = out_ref.shape[3]
    line = lax.axis_index("grp")
    first, start = window_of(line, width, noise.shape[3], span)
    copies = window_copies(noise, noise_ref, start, sem)
    for copy in copies:
        copy.start()
    band = spanwise_band(first - start, span, width)
    for c in range(comps):
        copies[c].wait()
        high, low = split(noise_ref[c].reshape(count * depth, span))
        along = dot(jnp.concatenate([high, low, high], axis=1), band)
        out_ref[c] = along.reshape(count, depth, width)


def filter_kernel(whole, along_hbm, rim, after, previous, decay_ref, factor_ref, mean_ref,
                    out_ref, planes_ref, prev_ref, along_ref, rim_ref, sem):
    del after
    comps, count, depth, width = along_ref.shape
    line = lax.axis_index("grp")
    first = part_of(line) * width
    before = previous_copy(previous, prev_ref, first, sem.at[0])
    rim_copy = pltpu.make_async_copy(rim, rim_ref, sem.at[1])
    along_copies = [
        pltpu.make_async_copy(along_hbm.at[c], along_ref.at[c], sem.at[2 + c])
        for c in range(comps)
    ]
    for copy in [rim_copy, before] + along_copies:
        copy.start()
    groups = LANES // HALF
    rows = depth // groups
    rim_at = jnp.where(line == 2, whole, -HALF) - first
    hrow = lax.broadcasted_iota(jnp.int32, (LANES, width), 0)
    hcol = lax.broadcasted_iota(jnp.int32, (LANES, width), 1)
    bands = []
    for q in range(groups):
        cell = hrow - HALF * q
        value = weights(cell + rim_at - hcol)
        high, low = split(jnp.where((cell >= 0) & (cell < HALF), value, 0.0))
        bands.append(jnp.concatenate([high, high, low], axis=0))
    band = jnp.concatenate(bands, axis=1)

    rim_copy.wait()

    def along(c):
        along_copies[c].wait()
        high, low = split(rim_ref[c].reshape(count * rows, LANES))
        part = dot(jnp.concatenate([high, low, high], axis=1), band)
        part = part.reshape(count, rows, groups * width)
        extra = [part[:, :, width * q : width * (q + 1)] for q in range(groups)]
        return along_ref[c] + jnp.concatenate(extra, axis=1)

    inflow_planes(along, before, decay_ref, factor_ref, mean_ref, out_ref, planes_ref, prev_ref)


def previous_copy(previous, prev_ref, first, sem):
    width = prev_ref.shape[2]
    if width % LANES == 0:
        previous = previous.at[:, :, pl.ds(pl.multiple_of(first, LANES), width)]
    return pltpu.make_async_copy(previous, prev_ref, sem)


def inflow_planes(along, before, decay_ref, factor_ref, mean_ref, out_ref, planes_ref, prev_ref):
    comps, count, depth, width = planes_ref.shape
    zrow = lax.broadcasted_iota(jnp.int32, (depth, depth), 0)
    zcol = lax.broadcasted_iota(jnp.int32, (depth, depth), 1)
    zh, zl = split(weights(zrow - zcol))
    zband = jnp.concatenate([zh, zh, zl], axis=1)
    for c in range(comps):
        value = along(c)
        wide = jnp.concatenate([value[p] for p in range(count)], axis=1)
        yh, yl = split(wide)
        smooth = dot(zband, jnp.concatenate([yh, yl, yh], axis=0))
        if c == 0:
            before.wait()
        dec = column(decay_ref, c, width)
        scale = jnp.sqrt(1.0 - dec * dec)
        carried = prev_ref[c]
        for p in range(count):
            carried = dec * carried + scale * smooth[:, p * width : (p + 1) * width]
            planes_ref[c, p] = carried
    owners = out_ref.shape[0]
    slab = depth // owners

    def put(c, p, value):
        for d in range(owners):
            out_ref[d, c, p] = value[slab * d : slab * (d + 1)]

    mean = column(mean_ref, 0, width)
    factor = [column(factor_ref, i, width) for i in range(6)]
    for p in range(count):
        a, b, d = planes_ref[0, p], planes_ref[1, p], planes_ref[2, p]
        put(0, p, mean + factor[0] * a)
        put(1, p, factor[1] * a + factor[2] * b)
        put(2, p, factor[3] * a + factor[4] * b + factor[5] * d)


def sides(near, far):
    even = lax.rem(lax.axis_index("grp"), 2) == 0
    return [(even, far, near), (jnp.logical_not(even), near, far)]


def corners_kernel(near, far, after, up_ref, dn_ref, sem):
    del after
    slab = near.shape[2]

    def rows(left, right):
        copies = []
        for ref, z in ((up_ref, slab - 1), (dn_ref, 0)):
            for i, (face, x) in enumerate(((left, 1), (right, 0))):
                for c in range(3):
                    copies.append(
                        pltpu.make_async_copy(face.at[c, x, z], ref.at[c, i], sem.at[len(copies)])
                    )
        return copies

    for condition, left, right in sides(near, far):

        @pl.when(condition)
        def _(left=left, right=right):
            run_copies(rows(left, right))


def inflow_faces_kernel(places, *refs):
    pieces = refs[:-3]
    dn, up, sem = refs[-3:]
    copies = []
    for piece, (source, part, parts) in zip(pieces, places):
        slab, width = piece.shape[3:]
        for s in range(piece.shape[0]):
            at = ((source + s) * parts + part) * width
            for j in range(2):
                for ref, z in ((dn, j), (up, slab - 2 + j)):
                    copies.append(
                        pltpu.make_async_copy(
                            piece.at[s, :, :, z],
                            ref.at[:, j, :, pl.ds(at, width)],
                            sem.at[len(copies)],
                        )
                    )

    @pl.when(lax.axis_index("grp") == 0)
    def _():
        run_copies(copies)


A = VISCOSITY * TIME_STEP
H = 0.5 * TIME_STEP
B = 1.0 - 6.0 * A
BLOCK = 512


def combine(scale, cs, xp, xn, zp, zn, yp, yn):
    a, h, b = A * scale, H * scale, B * scale
    cu, cw, cv = h * cs[0], h * cs[1], h * cs[2]
    out = []
    for i in range(3):
        total = xn[i] * (a - cu) + xp[i] * (a + cu)
        total = total + (zn[i] * (a - cw) + zp[i] * (a + cw))
        total = total + (yn[i] * (a - cv) + yp[i] * (a + cv))
        out.append(total + b * cs[i])
    return out


def spanwise(load, at, width, span):
    centre = load(at, width)
    wide = jnp.concatenate(
        [load((at - LANES) % span, LANES), centre, load((at + width) % span, LANES)], axis=1
    )
    total = width + 2 * LANES
    before = pltpu.roll(wide, 1, 1)[:, LANES : LANES + width]
    after = pltpu.roll(wide, total - 1, 1)[:, LANES : LANES + width]
    return centre, before, after


def main_block(scale, field, x, zb, za, zrow, at, width, span):
    top = lax.broadcasted_iota(jnp.int32, (SUB, width), 0)
    cs, xp, xn, zp, zn, yp, yn = [], [], [], [], [], [], []
    for c in range(3):
        centre, before, after = spanwise(
            lambda l, w, c=c: field[c, x, :, pl.ds(l, w)], at, width, span
        )
        cs.append(centre)
        yp.append(before)
        yn.append(after)
        xp.append(field[c, x - 1, :, pl.ds(at, width)])
        xn.append(field[c, x + 1, :, pl.ds(at, width)])
        low = jnp.broadcast_to(zb[c, pl.ds(zrow, 1), pl.ds(at, width)], (SUB, width))
        high = jnp.broadcast_to(za[c, pl.ds(zrow, 1), pl.ds(at, width)], (SUB, width))
        zp.append(jnp.where(top == 0, low, pltpu.roll(centre, 1, 0)))
        zn.append(jnp.where(top == SUB - 1, high, pltpu.roll(centre, SUB - 1, 0)))
    return combine(scale, cs, xp, xn, zp, zn, yp, yn)


def edge_rows(near, before, after, out, keep, begin, groups, span):
    def block(i, _):
        at = pl.multiple_of(i * BLOCK, BLOCK)
        left = pl.multiple_of(lax.rem(at + span - LANES, span), LANES)
        right = pl.multiple_of(lax.rem(at + BLOCK, span), LANES)
        for g in range(begin, groups):
            cs, xp, xn, zp, zn, yp, yn = [], [], [], [], [], [], []
            for c in range(3):
                r = SUB * (g + 1)
                centre = near[c, r : r + SUB, pl.ds(at, BLOCK)]
                wide = jnp.concatenate(
                    [
                        near[c, r : r + SUB, pl.ds(left, LANES)],
                        centre,
                        near[c, r : r + SUB, pl.ds(right, LANES)],
                    ],
                    axis=1,
                )
                total = BLOCK + 2 * LANES
                cs.append(centre)
                yp.append(pltpu.roll(wide, 1, 1)[:, LANES : LANES + BLOCK])
                yn.append(pltpu.roll(wide, total - 1, 1)[:, LANES : LANES + BLOCK])
                xp.append(near[c, r - 1 : r - 1 + SUB, pl.ds(at, BLOCK)])
                xn.append(near[c, r + 1 : r + 1 + SUB, pl.ds(at, BLOCK)])
                zp.append(before[c, SUB * g : SUB * (g + 1), pl.ds(at, BLOCK)])
                zn.append(after[c, SUB * g : SUB * (g + 1), pl.ds(at, BLOCK)])
            new = combine(1.0, cs, xp, xn, zp, zn, yp, yn)
            for c in range(3):
                out[c, SUB * (g + 1) : SUB * (g + 2), pl.ds(at, BLOCK)] = jnp.where(
                    keep, new[c], 0.0
                )
        return 0

    lax.fori_loop(0, span // BLOCK, block, 0)


def section_plane(x, start, sect, nb, na, span, keep=None):
    for at in range(0, span, BLOCK):
        new = main_block(1.0, start, x + 2, nb, na, SUB + x, at, BLOCK, span)
        for c in range(3):
            value = new[c] if keep is None else jnp.where(keep, new[c], 0.0)
            sect[c, x + 1, :, at : at + BLOCK] = value


def second_plane(x, start, sect, eb, ea, out, span):
    for at in range(0, span, BLOCK):
        new = main_block(0.5, sect, x + 1, eb, ea, SUB + x, at, BLOCK, span)
        for c in range(3):
            out[c, x, :, at : at + BLOCK] = new[c] + 0.5 * start[c, x + 2, :, at : at + BLOCK]


def rows_scratch(cells, span):
    shift = [
        pltpu.VMEM((3, cells + 2 * SUB, span), F32),
        pltpu.VMEM((3, cells + 2 * SUB, span), F32),
    ]
    side = [pltpu.VMEM((3, cells, span), F32)] * 4
    return shift + side + shift


def run_copies(copies):
    for copy in copies:
        copy.start()
    for copy in copies:
        copy.wait()


def roles(rows, ranks):
    r, g = lax.axis_index("grp"), lax.axis_index("gx")
    return g > 0, g < ranks - 1, r > 0, r < rows - 1, r == 0


def row_pieces(faces, first, nb, na, b2, b0, a0, a2):
    count = faces[0].shape[2]
    return [
        (faces[i].at[:, j], ref.at[:, pl.ds(at + first, count)])
        for i, j, ref, at in ((2, 1, nb, SUB), (3, 0, na, SUB), (2, 0, b2, 0), (3, 1, a2, 0),
                              (0, 0, b0, 0), (1, 1, a0, 0))
    ]


def own_kernel(rows, ranks, vel, *refs):
    (near, far, up_corners, dn_corners, dn_all, up_all, b_all, a_all, dn_hi, up_hi, b_hi, a_hi,
     out_hbm, start, sect, out, nb, na, b2, b0, a0, a2, eb, ea, corner, sem, out_sem) = refs
    cells = vel.shape[1]
    low = cells - dn_hi.shape[2]
    span = vel.shape[3]
    has_before, has_after, has_left, has_right, is_first = roles(rows, ranks)
    first = jnp.where(is_first, low + 2, 0)
    always = [
        (vel.at[:, pl.ds(low, cells - low)], start.at[:, pl.ds(2 + low, cells - low)]),
        (up_corners, corner.at[0]),
        (dn_corners, corner.at[1]),
    ]
    always = [pltpu.make_async_copy(p, q, sem.at[i]) for i, (p, q) in enumerate(always)]
    for copy in always:
        copy.start()

    def rest(pieces):
        run_copies(
            [
                pltpu.make_async_copy(p, q, sem.at[len(always) + i])
                for i, (p, q) in enumerate(pieces)
            ]
        )

    for condition, left, right in sides(near, far):

        @pl.when(condition)
        def _(left=left, right=right):
            rest(
                [(left, start.at[:, pl.ds(0, 2)]), (right, start.at[:, pl.ds(cells + 2, 2)])]
            )

    @pl.when(is_first)
    def _():
        rest(row_pieces((dn_hi, up_hi, b_hi, a_hi), low, nb, na, b2, b0, a0, a2))

    @pl.when(jnp.logical_not(is_first))
    def _():
        pieces = row_pieces((dn_all, up_all, b_all, a_all), 0, nb, na, b2, b0, a0, a2)
        rest(pieces + [(vel.at[:, pl.ds(0, low)], start.at[:, pl.ds(2, low)])])

    for copy in always:
        copy.wait()

    @pl.when(jnp.logical_not(has_right))
    def _():
        for c in range(3):
            start[c, cells + 2] = jnp.zeros((SUB, span), F32)
            for i in range(2):
                corner[i, c, 1:2, :] = jnp.zeros((1, span), F32)

    for c in range(3):
        nb[c, SUB - 1 : SUB, :] = corner[0, c, 0:1, :]
        nb[c, SUB + cells : SUB + cells + 1, :] = corner[0, c, 1:2, :]
        na[c, SUB - 1 : SUB, :] = corner[1, c, 0:1, :]
        na[c, SUB + cells : SUB + cells + 1, :] = corner[1, c, 1:2, :]
    groups = cells // SUB

    @pl.when(jnp.logical_not(is_first))
    def _():
        edge_rows(nb, b2, b0, eb, has_before, 0, low // SUB, span)
        edge_rows(na, a0, a2, ea, has_after, 0, low // SUB, span)

    edge_rows(nb, b2, b0, eb, has_before, low // SUB, groups, span)
    edge_rows(na, a0, a2, ea, has_after, low // SUB, groups, span)

    def make(x, keep=None):
        section_plane(x, start, sect, nb, na, span, keep)

    def body(x, _):
        keep = jnp.logical_or(
            jnp.logical_and(x >= 0, x < cells),
            jnp.logical_or(jnp.logical_and(x < 0, has_left), jnp.logical_and(x >= cells, has_right)),
        )
        make(x, keep)

        @pl.when(x >= first + 1)
        def _():
            second_plane(x - 1, start, sect, eb, ea, out, span)
            pltpu.make_async_copy(out.at[:, x - 1], out_hbm.at[:, x - 1], out_sem.at[x - 1]).start()

        return 0

    lax.fori_loop(first - 1, cells + 1, body, 0)

    def drain(x, _):
        pltpu.make_async_copy(out.at[:, x], out_hbm.at[:, x], out_sem.at[x]).wait()
        return 0

    lax.fori_loop(first, cells, drain, 0)


def inflow_kernel(rows, ranks, places, vel, *refs):
    parts, refs = refs[:-23], refs[-23:]
    dn_in, up_in, b_in, a_in, dn_hi, up_hi, b_hi, a_hi, _, out_hbm = refs[:10]
    start, sect, out, nb, na, b2, b0, a0, a2, eb, ea, sem, out_sem = refs[10:]
    low = dn_in.shape[2]
    span = vel.shape[3]
    reach = out.shape[1]
    cells = b2.shape[1]
    has_before, has_after, _, _, is_first = roles(rows, ranks)

    @pl.when(is_first)
    def _():
        pieces = [(vel.at[:, pl.ds(low, 4)], start.at[:, pl.ds(low + 2, 4)])]
        for piece, (source, part, many) in zip(parts, places):
            width = piece.shape[4]
            for s in range(piece.shape[0]):
                at = ((source + s) * many + part) * width
                pieces.append((piece.at[s], start.at[:, pl.ds(2, low), :, pl.ds(at, width)]))
        for lo, hi, j, ref, first in (
            (b_in, b_hi, 1, nb, SUB),
            (a_in, a_hi, 0, na, SUB),
            (b_in, b_hi, 0, b2, 0),
            (a_in, a_hi, 1, a2, 0),
            (dn_in, dn_hi, 0, b0, 0),
            (up_in, up_hi, 1, a0, 0),
        ):
            pieces.append((lo.at[:, j], ref.at[:, pl.ds(first, low)]))
            pieces.append((hi.at[:, j], ref.at[:, pl.ds(first + low, cells - low)]))
        copies = [
            pltpu.make_async_copy(src, dst, sem.at[i]) for i, (src, dst) in enumerate(pieces)
        ]
        for copy in copies:
            copy.start()
        zero = jnp.zeros((SUB, span), F32)
        for c in range(3):
            start[c, 1] = zero
            sect[c, 0] = zero
            for ref in (nb, na):
                ref[c, 0:SUB, :] = zero
                ref[c, SUB + cells :, :] = zero
        for copy in copies:
            copy.wait()
        groups = cells // SUB
        edge_rows(nb, b2, b0, eb, has_before, 0, groups, span)
        edge_rows(na, a0, a2, ea, has_after, 0, groups, span)
        section_plane(0, start, sect, nb, na, span)

        def body(x, _):
            section_plane(x + 1, start, sect, nb, na, span)
            second_plane(x, start, sect, eb, ea, out, span)
            pltpu.make_async_copy(out.at[:, x], out_hbm.at[:, x], out_sem.at[x]).start()
            return 0

        lax.fori_loop(0, reach, body, 0)

        def drain(x, _):
            pltpu.make_async_copy(out.at[:, x], out_hbm.at[:, x], out_sem.at[x]).wait()
            return 0

        lax.fori_loop(0, reach, drain, 0)


def call(kernel, out_shape, out_specs, in_specs, scratch, estimate, alias=None):
    def run(*args):
        return pl.pallas_call(
            kernel,
            out_shape=out_shape,
            in_specs=in_specs,
            out_specs=out_specs,
            scratch_shapes=scratch,
            input_output_aliases=alias or {},
            compiler_params=params(),
            cost_estimate=estimate,
        )(*args)

    return run


def local(velocity, noise, previous, decay, stress_factor, mean_profile):
    rows = lax.axis_size("grp")
    ranks = lax.axis_size("gx")
    comps, count, depth, span_local = noise.shape
    cells, slab, span = velocity.shape[1:]
    width = span_local // PARTS
    low = count
    high = cells - low
    dma = pltpu.SemaphoreType.DMA

    def along_gx(array, step, lines, idlers=()):
        pairs = idle(idlers) + [
            (r * ranks + i, r * ranks + i + step)
            for r in lines
            for i in range(ranks)
            if 0 <= i + step < ranks
        ]
        return lax.ppermute(array, ("grp", "gx"), pairs)

    packed = jax.ShapeDtypeStruct((comps, count, depth * HALF // LANES, LANES), F32)
    face = jax.ShapeDtypeStruct((3, 2, low, span), F32)
    face_hi = jax.ShapeDtypeStruct((3, 2, high, span), F32)
    xface = jax.ShapeDtypeStruct((3, 2, slab, span), F32)
    full = jax.ShapeDtypeStruct(velocity.shape, F32)
    rim_out = call(
        first_kernel,
        packed,
        VMEM,
        [ANY],
        [pltpu.VMEM((comps, count, depth, LANES), F32), dma((comps,))],
        cost(0, noise.size),
    )(noise)

    def idle(lines):
        return [(r * ranks + i, r * ranks + (i ^ 1)) for r in lines for i in range(ranks)]

    def across(array, moves, idlers):
        pairs = [(a * ranks + i, b * ranks + i) for a, b in moves for i in range(ranks)]
        return lax.ppermute(array, ("grp", "gx"), pairs + idle(idlers))

    pairs = idle([r for r in range(rows) if r not in (1, 2)])
    for line, step in ((1, 1), (2, -1)):
        pairs += [(line * ranks + i, line * ranks + (i + step) % ranks) for i in range(ranks)]
    rim = lax.ppermute(rim_out, ("grp", "gx"), pairs)
    everyone = range(rows)
    evens = range(0, rows - 1, 2)
    odds = range(1, rows - 1, 2)
    lone = [0] + ([rows - 1] if rows % 2 == 0 else [])

    window = min(span_local, LANES * (-(-(width + 2 * HALF) // LANES) + 1))
    made_shape = jax.ShapeDtypeStruct((ranks, comps, count, depth // ranks, width), F32)

    windowed = pltpu.VMEM((comps, count, depth, window), F32)

    def make(kernel, inputs, specs, scratch):
        prev = previous
        if width % LANES:
            at = part_of(lax.axis_index("grp")) * width
            prev = lax.dynamic_slice_in_dim(previous, at, width, 2)
        return call(
            kernel,
            made_shape,
            VMEM,
            specs + [ANY, VMEM, VMEM, VMEM],
            [
                pltpu.VMEM((comps, count, depth, width), F32),
                pltpu.VMEM((comps, depth, width), F32),
            ]
            + scratch,
            cost(6 * noise.size * width, 4 * noise.size),
        )(*inputs, prev, decay, stress_factor, mean_profile[None])

    near_out, far_out = call(
        xfaces_kernel, [xface, xface], [VMEM] * 2, [ANY] * 2, [dma((2,))], cost(0, velocity.size)
    )(velocity, rim_out)
    far = across(far_out, [p for i in odds for p in ((i, i + 1), (i + 1, i))], lone)
    along = call(
        along_kernel,
        jax.ShapeDtypeStruct((comps, count, depth, width), F32),
        VMEM,
        [ANY],
        [windowed, dma((comps,))],
        cost(6 * noise.size * width, 4 * noise.size),
    )(noise)
    kernel_a = functools.partial(filter_kernel, span_local)
    made_a = make(
        kernel_a, [along, rim, near_out], [ANY] * 3,
        [
            pltpu.VMEM((comps, count, depth, width), F32),
            pltpu.VMEM(packed.shape, F32),
            dma((comps + 2,)),
        ],
    )
    got_a = lax.all_to_all(made_a, "gx", 0, 0, tiled=True)

    near = across(near_out, [p for i in evens for p in ((i, i + 1), (i + 1, i))], [])
    face_all = jax.ShapeDtypeStruct((3, 2, cells, span), F32)
    dn_all, up_all, dn_hi, up_hi = call(
        zfaces_kernel, [face_all, face_all, face_hi, face_hi], [VMEM] * 4, [ANY] * 2,
        [dma((12,))], cost(0, velocity.size),
    )(velocity, made_a)
    others = range(1, rows)
    b_hi = along_gx(up_hi, 1, [0], others)
    a_hi = along_gx(dn_hi, -1, [0], others)

    half = ranks // 2
    side = lax.ppermute(got_a[half:], "grp", [(3, 1)])
    hop_1 = lax.ppermute(got_a, "grp", [(1, 0)])
    hop_2 = lax.ppermute(got_a, "grp", [(2, 0)])
    hop_3 = lax.ppermute(got_a[:half], "grp", [(3, 0)])

    b_all = along_gx(up_all, 1, others)
    a_all = along_gx(dn_all, -1, others)

    mark = call(
        mark_kernel, jax.ShapeDtypeStruct((SUB, LANES), F32), VMEM, [ANY], [], cost(0, 1024)
    )(made_a)
    pair = jax.ShapeDtypeStruct((3, 2, span), F32)
    up_corner, dn_corner = call(
        corners_kernel, [pair, pair], [VMEM] * 2, [ANY] * 3, [dma((12,))], cost(0, 24 * span)
    )(near, far, mark)
    up_corners = along_gx(up_corner, 1, everyone)
    dn_corners = along_gx(dn_corner, -1, everyone)

    def fields(planes):
        return [
            pltpu.VMEM((3, planes + 4, slab, span), F32),
            pltpu.VMEM((3, planes + 2, slab, span), F32),
            pltpu.VMEM((3, planes, slab, span), F32),
        ]

    hop_4 = lax.ppermute(side, "grp", [(1, 0)])
    own = call(
        functools.partial(own_kernel, rows, ranks),
        full,
        ANY,
        [ANY] * 13,
        fields(cells)
        + rows_scratch(cells, span)
        + [pltpu.VMEM((2, 3, 2, span), F32), dma((12,)), dma((cells,))],
        cost(50 * velocity.size, 8 * velocity.size),
    )(velocity, near, far, up_corners, dn_corners, dn_all, up_all, b_all, a_all, dn_hi, up_hi, b_hi,
      a_hi)

    parts = [hop_1, got_a, hop_3, hop_4, hop_2]
    places = [(0, 0, PARTS), (0, 1, PARTS), (0, 2, PARTS), (half, 2, PARTS), (0, 3, PARTS)]
    if width != LANES:
        joined = [hop_1, got_a, jnp.concatenate([hop_3, hop_4], axis=0), hop_2]
        joined = jnp.concatenate(joined, axis=4)
        parts = [joined[..., at : at + LANES] for at in range(0, span_local, LANES)]
        places = [(0, i, len(parts)) for i in range(len(parts))]
    many = len(parts)
    dn_in, up_in = call(
        functools.partial(inflow_faces_kernel, places),
        [face, face],
        [VMEM] * 2,
        [ANY] * many,
        [dma((4 * sum(p.shape[0] for p in parts),))],
        cost(0, 8 * noise.size),
    )(*parts)
    b_in = along_gx(up_in, 1, [0])
    a_in = along_gx(dn_in, -1, [0])

    reach = low + 2
    return call(
        functools.partial(inflow_kernel, rows, ranks, places),
        full,
        ANY,
        [ANY] * (many + 10),
        fields(reach)
        + rows_scratch(low + high, span)
        + [dma((sum(p.shape[0] for p in parts) + 13,)), dma((reach,))],
        cost(30 * velocity.size, 5 * velocity.size),
        {many + 9: 0},
    )(velocity, *parts, dn_in, up_in, b_in, a_in, dn_hi, up_hi, b_hi, a_hi, own)


def solution(mesh):
    placed = (
        P(None, "grp", "gx", None),
        P(None, None, None, "gx"),
        P(None, None, "gx"),
        P(),
        P(),
        P(),
    )

    return jax.shard_map(
        local, mesh=mesh, in_specs=placed, out_specs=P(None, "grp", "gx", None), check_vma=False
    )
```

```python
import functools
import math

import jax
import jax.numpy as jnp
from jax import lax
from jax.experimental import pallas as pl
from jax.experimental.pallas import tpu as pltpu
from jax.sharding import PartitionSpec as P


HALF = 32
TIME_STEP = 0.15
VISCOSITY = 0.2
LANES = 128
SUB = 8
PARTS = 4
VMEM_LIMIT = 60 * 1024 * 1024

ANY = pl.BlockSpec(memory_space=pltpu.HBM)
VMEM = pl.BlockSpec(memory_space=pltpu.VMEM)
F32 = jnp.float32


def params():
    return pltpu.CompilerParams(vmem_limit_bytes=VMEM_LIMIT)


def cost(flops, nbytes):
    return pl.CostEstimate(flops=flops, bytes_accessed=nbytes, transcendentals=0)


def kernel_norm():
    length = HALF / 2.0
    total = sum(
        math.exp(-math.pi * k * k / (2.0 * length * length)) ** 2 for k in range(-HALF, HALF + 1)
    )
    return math.sqrt(total)


def weights(offset):
    length = HALF / 2.0
    off = offset.astype(F32)
    value = jnp.exp(off * off * (-math.pi / (2.0 * length * length))) * (1.0 / kernel_norm())
    return jnp.where(jnp.abs(offset) <= HALF, value, 0.0)


def split(x):
    high = x.astype(jnp.bfloat16)
    low = (x - high.astype(F32)).astype(jnp.bfloat16)
    return high, low


def dot(a, b):
    return jnp.dot(a, b, preferred_element_type=F32)


def first_kernel(noise, vel, rim_ref, near_ref, far_ref, edge, sem):
    comps, count, depth, span = noise.shape
    groups = LANES // HALF
    rows = depth // groups
    use_left = lax.axis_index("grp") == 2
    at = pl.multiple_of(jnp.where(use_left, 0, span - LANES), LANES)
    copies = [
        pltpu.make_async_copy(noise.at[c, :, :, pl.ds(at, LANES)], edge.at[c], sem.at[c])
        for c in range(comps)
    ]
    for copy in copies:
        copy.start()
    cells = vel.shape[1]
    even = lax.rem(lax.axis_index("grp"), 2) == 0
    x = jnp.where(even, cells - 2, 0)
    faces = [
        pltpu.make_async_copy(vel.at[:, pl.ds(x, 2)], near_ref, sem.at[comps]),
        pltpu.make_async_copy(vel.at[:, pl.ds(cells - 2 - x, 2)], far_ref, sem.at[comps + 1]),
    ]
    for copy in faces:
        copy.start()
    lane = lax.broadcasted_iota(jnp.int32, (count, rows, LANES), 2)
    for c in range(comps):
        copies[c].wait()
        result = None
        for q in range(groups):
            piece = edge[c, :, rows * q : rows * (q + 1), :]
            to_left = piece if q == 0 else pltpu.roll(piece, HALF * q, 2)
            to_right = pltpu.roll(piece, (HALF * (q + 1)) % LANES, 2) if (q + 1) % groups else piece
            piece = jnp.where(use_left, to_left, to_right)
            result = piece if q == 0 else jnp.where(lane >= HALF * q, piece, result)
        rim_ref[c] = result
    for copy in faces:
        copy.wait()


def face_copies(vel, first, cells, dn, up, sem, at):
    slab = vel.shape[2]
    copies = []
    for c in range(3):
        for j in range(2):
            for ref, z in ((dn, j), (up, slab - 2 + j)):
                copies.append(
                    pltpu.make_async_copy(
                        vel.at[c, pl.ds(first, cells), z], ref.at[c, j], sem.at[at + len(copies)]
                    )
                )
    return copies


def zfaces_kernel(vel, after, all_dn, all_up, high_dn, high_up, sem):
    del after
    cells, high = all_dn.shape[2], high_dn.shape[2]
    is_first = lax.axis_index("grp") == 0

    @pl.when(is_first)
    def _():
        run_copies(face_copies(vel, cells - high, high, high_dn, high_up, sem, 0))

    @pl.when(jnp.logical_not(is_first))
    def _():
        run_copies(face_copies(vel, 0, cells, all_dn, all_up, sem, 0))


def mark_kernel(after, out_ref):
    del after
    out_ref[...] = jnp.zeros_like(out_ref)


def column(ref, c, width):
    depth = ref.shape[1]
    row = lax.broadcasted_iota(jnp.int32, (depth, depth), 0)
    col = lax.broadcasted_iota(jnp.int32, (depth, depth), 1)
    value = jnp.where(row == col, jnp.broadcast_to(ref[c : c + 1, :], (depth, depth)), 0.0)
    return jnp.broadcast_to(jnp.sum(value, axis=1, keepdims=True), (depth, width))


def part_of(line):
    return jnp.where(line == 0, 1, jnp.where(line == 1, 0, jnp.where(line == 2, PARTS - 1, 2)))


def window_of(line, width, whole, span):
    first = part_of(line) * width
    start = jnp.minimum(jnp.maximum((first - HALF) // LANES * LANES, 0), whole - span)
    return first, pl.multiple_of(start, LANES)


def spanwise_band(base, span, width):
    row = lax.broadcasted_iota(jnp.int32, (span, width), 0)
    col = lax.broadcasted_iota(jnp.int32, (span, width), 1)
    high, low = split(weights(row - col - base))
    return jnp.concatenate([high, high, low], axis=0)


def window_copies(noise, noise_ref, start, sem):
    comps, _, _, span = noise_ref.shape
    return [
        pltpu.make_async_copy(noise.at[c, :, :, pl.ds(start, span)], noise_ref.at[c], sem.at[c])
        for c in range(comps)
    ]


def along_kernel(noise, out_ref, noise_ref, sem):
    comps, count, depth, span = noise_ref.shape
    width = out_ref.shape[3]
    line = lax.axis_index("grp")
    first, start = window_of(line, width, noise.shape[3], span)
    copies = window_copies(noise, noise_ref, start, sem)
    for copy in copies:
        copy.start()
    band = spanwise_band(first - start, span, width)
    for c in range(comps):
        copies[c].wait()
        high, low = split(noise_ref[c].reshape(count * depth, span))
        along = dot(jnp.concatenate([high, low, high], axis=1), band)
        out_ref[c] = along.reshape(count, depth, width)


def filter_kernel(whole, along_hbm, rim, previous, decay_ref, factor_ref, mean_ref,
                    out_ref, planes_ref, prev_ref, along_ref, rim_ref, sem):
    comps, count, depth, width = along_ref.shape
    line = lax.axis_index("grp")
    first = part_of(line) * width
    before = previous_copy(previous, prev_ref, first, sem.at[0])
    rim_copy = pltpu.make_async_copy(rim, rim_ref, sem.at[1])
    along_copies = [
        pltpu.make_async_copy(along_hbm.at[c], along_ref.at[c], sem.at[2 + c])
        for c in range(comps)
    ]
    for copy in [rim_copy, before] + along_copies:
        copy.start()
    groups = LANES // HALF
    rows = depth // groups
    rim_at = jnp.where(line == 2, whole, -HALF) - first
    hrow = lax.broadcasted_iota(jnp.int32, (LANES, width), 0)
    hcol = lax.broadcasted_iota(jnp.int32, (LANES, width), 1)
    bands = []
    for q in range(groups):
        cell = hrow - HALF * q
        value = weights(cell + rim_at - hcol)
        high, low = split(jnp.where((cell >= 0) & (cell < HALF), value, 0.0))
        bands.append(jnp.concatenate([high, high, low], axis=0))
    band = jnp.concatenate(bands, axis=1)

    rim_copy.wait()

    def along(c):
        along_copies[c].wait()
        high, low = split(rim_ref[c].reshape(count * rows, LANES))
        part = dot(jnp.concatenate([high, low, high], axis=1), band)
        part = part.reshape(count, rows, groups * width)
        extra = [part[:, :, width * q : width * (q + 1)] for q in range(groups)]
        return along_ref[c] + jnp.concatenate(extra, axis=1)

    inflow_planes(along, before, decay_ref, factor_ref, mean_ref, out_ref, planes_ref, prev_ref)


def previous_copy(previous, prev_ref, first, sem):
    width = prev_ref.shape[2]
    if width % LANES == 0:
        previous = previous.at[:, :, pl.ds(pl.multiple_of(first, LANES), width)]
    return pltpu.make_async_copy(previous, prev_ref, sem)


def inflow_planes(along, before, decay_ref, factor_ref, mean_ref, out_ref, planes_ref, prev_ref):
    comps, count, depth, width = planes_ref.shape
    zrow = lax.broadcasted_iota(jnp.int32, (depth, depth), 0)
    zcol = lax.broadcasted_iota(jnp.int32, (depth, depth), 1)
    zh, zl = split(weights(zrow - zcol))
    zband = jnp.concatenate([zh, zh, zl], axis=1)
    for c in range(comps):
        value = along(c)
        wide = jnp.concatenate([value[p] for p in range(count)], axis=1)
        yh, yl = split(wide)
        smooth = dot(zband, jnp.concatenate([yh, yl, yh], axis=0))
        if c == 0:
            before.wait()
        dec = column(decay_ref, c, width)
        scale = jnp.sqrt(1.0 - dec * dec)
        carried = prev_ref[c]
        for p in range(count):
            carried = dec * carried + scale * smooth[:, p * width : (p + 1) * width]
            planes_ref[c, p] = carried
    owners = out_ref.shape[0]
    slab = depth // owners

    def put(c, p, value):
        for d in range(owners):
            out_ref[d, c, p] = value[slab * d : slab * (d + 1)]

    mean = column(mean_ref, 0, width)
    factor = [column(factor_ref, i, width) for i in range(6)]
    for p in range(count):
        a, b, d = planes_ref[0, p], planes_ref[1, p], planes_ref[2, p]
        put(0, p, mean + factor[0] * a)
        put(1, p, factor[1] * a + factor[2] * b)
        put(2, p, factor[3] * a + factor[4] * b + factor[5] * d)


def sides(near, far, detour):
    line = lax.axis_index("grp")
    even = lax.rem(line, 2) == 0
    odd = (jnp.logical_not(even), near, far)
    if detour is None:
        return [(even, far, near), odd]
    return [(line == 2, detour, near), (jnp.logical_and(even, line != 2), far, near), odd]


def corners_kernel(*refs):
    near, far, *detour, _, up_ref, dn_ref, sem = refs
    slab = near.shape[2]

    def rows(left, right):
        copies = []
        for ref, z in ((up_ref, slab - 1), (dn_ref, 0)):
            for i, (face, x) in enumerate(((left, 1), (right, 0))):
                for c in range(3):
                    copies.append(
                        pltpu.make_async_copy(face.at[c, x, z], ref.at[c, i], sem.at[len(copies)])
                    )
        return copies

    for condition, left, right in sides(near, far, detour[0] if detour else None):

        @pl.when(condition)
        def _(left=left, right=right):
            run_copies(rows(left, right))


def inflow_faces_kernel(places, *refs):
    pieces = refs[:-3]
    dn, up, sem = refs[-3:]
    copies = []
    for piece, (source, part, parts) in zip(pieces, places):
        slab, width = piece.shape[3:]
        for s in range(piece.shape[0]):
            at = ((source + s) * parts + part) * width
            for j in range(2):
                for ref, z in ((dn, j), (up, slab - 2 + j)):
                    copies.append(
                        pltpu.make_async_copy(
                            piece.at[s, :, :, z],
                            ref.at[:, j, :, pl.ds(at, width)],
                            sem.at[len(copies)],
                        )
                    )

    @pl.when(lax.axis_index("grp") == 0)
    def _():
        run_copies(copies)


A = VISCOSITY * TIME_STEP
H = 0.5 * TIME_STEP
B = 1.0 - 6.0 * A
BLOCK = 512


def combine(scale, cs, xp, xn, zp, zn, yp, yn):
    a, h, b = A * scale, H * scale, B * scale
    cu, cw, cv = h * cs[0], h * cs[1], h * cs[2]
    out = []
    for i in range(3):
        total = xn[i] * (a - cu) + xp[i] * (a + cu)
        total = total + (zn[i] * (a - cw) + zp[i] * (a + cw))
        total = total + (yn[i] * (a - cv) + yp[i] * (a + cv))
        out.append(total + b * cs[i])
    return out


def spanwise(load, at, width, span):
    centre = load(at, width)
    wide = jnp.concatenate(
        [load((at - LANES) % span, LANES), centre, load((at + width) % span, LANES)], axis=1
    )
    total = width + 2 * LANES
    before = pltpu.roll(wide, 1, 1)[:, LANES : LANES + width]
    after = pltpu.roll(wide, total - 1, 1)[:, LANES : LANES + width]
    return centre, before, after


def main_block(scale, field, x, zb, za, zrow, at, width, span):
    top = lax.broadcasted_iota(jnp.int32, (SUB, width), 0)
    cs, xp, xn, zp, zn, yp, yn = [], [], [], [], [], [], []
    for c in range(3):
        centre, before, after = spanwise(
            lambda l, w, c=c: field[c, x, :, pl.ds(l, w)], at, width, span
        )
        cs.append(centre)
        yp.append(before)
        yn.append(after)
        xp.append(field[c, x - 1, :, pl.ds(at, width)])
        xn.append(field[c, x + 1, :, pl.ds(at, width)])
        low = jnp.broadcast_to(zb[c, pl.ds(zrow, 1), pl.ds(at, width)], (SUB, width))
        high = jnp.broadcast_to(za[c, pl.ds(zrow, 1), pl.ds(at, width)], (SUB, width))
        zp.append(jnp.where(top == 0, low, pltpu.roll(centre, 1, 0)))
        zn.append(jnp.where(top == SUB - 1, high, pltpu.roll(centre, SUB - 1, 0)))
    return combine(scale, cs, xp, xn, zp, zn, yp, yn)


def edge_rows(near, before, after, out, keep, begin, groups, span):
    def block(i, _):
        at = pl.multiple_of(i * BLOCK, BLOCK)
        left = pl.multiple_of(lax.rem(at + span - LANES, span), LANES)
        right = pl.multiple_of(lax.rem(at + BLOCK, span), LANES)
        for g in range(begin, groups):
            cs, xp, xn, zp, zn, yp, yn = [], [], [], [], [], [], []
            for c in range(3):
                r = SUB * (g + 1)
                centre = near[c, r : r + SUB, pl.ds(at, BLOCK)]
                wide = jnp.concatenate(
                    [
                        near[c, r : r + SUB, pl.ds(left, LANES)],
                        centre,
                        near[c, r : r + SUB, pl.ds(right, LANES)],
                    ],
                    axis=1,
                )
                total = BLOCK + 2 * LANES
                cs.append(centre)
                yp.append(pltpu.roll(wide, 1, 1)[:, LANES : LANES + BLOCK])
                yn.append(pltpu.roll(wide, total - 1, 1)[:, LANES : LANES + BLOCK])
                xp.append(near[c, r - 1 : r - 1 + SUB, pl.ds(at, BLOCK)])
                xn.append(near[c, r + 1 : r + 1 + SUB, pl.ds(at, BLOCK)])
                zp.append(before[c, SUB * g : SUB * (g + 1), pl.ds(at, BLOCK)])
                zn.append(after[c, SUB * g : SUB * (g + 1), pl.ds(at, BLOCK)])
            new = combine(1.0, cs, xp, xn, zp, zn, yp, yn)
            for c in range(3):
                out[c, SUB * (g + 1) : SUB * (g + 2), pl.ds(at, BLOCK)] = jnp.where(
                    keep, new[c], 0.0
                )
        return 0

    lax.fori_loop(0, span // BLOCK, block, 0)


def section_plane(x, start, sect, nb, na, span, keep=None):
    for at in range(0, span, BLOCK):
        new = main_block(1.0, start, x + 2, nb, na, SUB + x, at, BLOCK, span)
        for c in range(3):
            value = new[c] if keep is None else jnp.where(keep, new[c], 0.0)
            sect[c, x + 1, :, at : at + BLOCK] = value


def second_plane(x, start, sect, eb, ea, out, span):
    for at in range(0, span, BLOCK):
        new = main_block(0.5, sect, x + 1, eb, ea, SUB + x, at, BLOCK, span)
        for c in range(3):
            out[c, x, :, at : at + BLOCK] = new[c] + 0.5 * start[c, x + 2, :, at : at + BLOCK]


def rows_scratch(cells, span):
    shift = [
        pltpu.VMEM((3, cells + 2 * SUB, span), F32),
        pltpu.VMEM((3, cells + 2 * SUB, span), F32),
    ]
    side = [pltpu.VMEM((3, cells, span), F32)] * 4
    return shift + side + shift


def begin(copies, condition=None):
    if condition is not None:
        pl.when(condition)(lambda: begin(copies))
        return
    for copy in copies:
        copy.start()


def finish(copies, condition=None):
    if condition is not None:
        pl.when(condition)(lambda: finish(copies))
        return
    for copy in copies:
        copy.wait()


def run_copies(copies):
    for copy in copies:
        copy.start()
    for copy in copies:
        copy.wait()


def roles(rows, ranks):
    r, g = lax.axis_index("grp"), lax.axis_index("gx")
    return g > 0, g < ranks - 1, r > 0, r < rows - 1, r == 0


def row_pieces(faces, first, nb, na, b2, b0, a0, a2):
    count = faces[0].shape[2]
    return [
        (faces[i].at[:, j], ref.at[:, pl.ds(at + first, count)])
        for i, j, ref, at in ((2, 1, nb, SUB), (3, 0, na, SUB), (2, 0, b2, 0), (3, 1, a2, 0),
                              (0, 0, b0, 0), (1, 1, a0, 0))
    ]


def own_kernel(rows, ranks, vel, *refs):
    near, far, *detour = refs[:-25]
    (up_corners, dn_corners, dn_all, up_all, b_all, a_all, dn_hi, up_hi, b_hi, a_hi, out_hbm,
     start, sect, out, nb, na, b2, b0, a0, a2, eb, ea, corner, sem, out_sem) = refs[-25:]
    cells = vel.shape[1]
    low = cells - dn_hi.shape[2]
    span = vel.shape[3]
    has_before, has_after, has_left, has_right, is_first = roles(rows, ranks)
    first = jnp.where(is_first, low + 2, 0)
    is_other = jnp.logical_not(is_first)
    left_at, right_at = start.at[:, pl.ds(0, 2)], start.at[:, pl.ds(cells + 2, 2)]
    rows_first = row_pieces((dn_hi, up_hi, b_hi, a_hi), low, nb, na, b2, b0, a0, a2)
    rows_other = row_pieces((dn_all, up_all, b_all, a_all), 0, nb, na, b2, b0, a0, a2)
    ends = [(up_corners, corner.at[0]), (dn_corners, corner.at[1])]
    main = [(vel.at[:, pl.ds(low, cells - low)], start.at[:, pl.ds(2 + low, cells - low)])]
    rest = [(vel.at[:, pl.ds(0, low)], start.at[:, pl.ds(2, low)])]

    def copies(pieces, at):
        return [pltpu.make_async_copy(p, q, sem.at[at + i]) for i, (p, q) in enumerate(pieces)]

    begin(copies(rows_first, 0), is_first)
    begin(copies(rows_other, 0), is_other)
    begin(copies(ends, 6))
    begin(copies(main, 8))
    for condition, left, right in sides(near, far, detour[0] if detour else None):
        begin(copies([(right, right_at)], 9), condition)
        begin(copies([(left, left_at)], 10), jnp.logical_and(condition, is_other))
    begin(copies(rest, 11), is_other)
    finish(copies(rows_first, 0), is_first)
    finish(copies(rows_other, 0), is_other)
    finish(copies(ends, 6))

    @pl.when(jnp.logical_not(has_right))
    def _():
        for c in range(3):
            for i in range(2):
                corner[i, c, 1:2, :] = jnp.zeros((1, span), F32)

    for c in range(3):
        nb[c, SUB - 1 : SUB, :] = corner[0, c, 0:1, :]
        nb[c, SUB + cells : SUB + cells + 1, :] = corner[0, c, 1:2, :]
        na[c, SUB - 1 : SUB, :] = corner[1, c, 0:1, :]
        na[c, SUB + cells : SUB + cells + 1, :] = corner[1, c, 1:2, :]
    groups = cells // SUB

    @pl.when(jnp.logical_not(is_first))
    def _():
        edge_rows(nb, b2, b0, eb, has_before, 0, low // SUB, span)
        edge_rows(na, a0, a2, ea, has_after, 0, low // SUB, span)

    edge_rows(nb, b2, b0, eb, has_before, low // SUB, groups, span)
    edge_rows(na, a0, a2, ea, has_after, low // SUB, groups, span)
    finish(copies(main, 8))
    finish(copies([(near, right_at)], 9))
    finish(copies([(near, left_at)], 10), is_other)
    finish(copies(rest, 11), is_other)

    @pl.when(jnp.logical_not(has_right))
    def _():
        for c in range(3):
            start[c, cells + 2] = jnp.zeros((SUB, span), F32)

    def make(x, keep=None):
        section_plane(x, start, sect, nb, na, span, keep)

    def body(x, _):
        keep = jnp.logical_or(
            jnp.logical_and(x >= 0, x < cells),
            jnp.logical_or(jnp.logical_and(x < 0, has_left), jnp.logical_and(x >= cells, has_right)),
        )
        make(x, keep)

        @pl.when(x >= first + 1)
        def _():
            second_plane(x - 1, start, sect, eb, ea, out, span)
            pltpu.make_async_copy(out.at[:, x - 1], out_hbm.at[:, x - 1], out_sem.at[x - 1]).start()

        return 0

    lax.fori_loop(first - 1, cells + 1, body, 0)

    def drain(x, _):
        pltpu.make_async_copy(out.at[:, x], out_hbm.at[:, x], out_sem.at[x]).wait()
        return 0

    lax.fori_loop(first, cells, drain, 0)


def inflow_kernel(rows, ranks, places, vel, *refs):
    parts, refs = refs[:-23], refs[-23:]
    dn_in, up_in, b_in, a_in, dn_hi, up_hi, b_hi, a_hi, _, out_hbm = refs[:10]
    start, sect, out, nb, na, b2, b0, a0, a2, eb, ea, sem, out_sem = refs[10:]
    low = dn_in.shape[2]
    span = vel.shape[3]
    reach = out.shape[1]
    cells = b2.shape[1]
    has_before, has_after, _, _, is_first = roles(rows, ranks)

    @pl.when(is_first)
    def _():
        edges = row_pieces((dn_in, up_in, b_in, a_in), 0, nb, na, b2, b0, a0, a2)
        edges += row_pieces((dn_hi, up_hi, b_hi, a_hi), low, nb, na, b2, b0, a0, a2)
        main = [(vel.at[:, pl.ds(low, 4)], start.at[:, pl.ds(low + 2, 4)])]
        for piece, (source, part, many) in zip(parts, places):
            width = piece.shape[4]
            for i in range(piece.shape[0]):
                at = ((source + i) * many + part) * width
                main.append((piece.at[i], start.at[:, pl.ds(2, low), :, pl.ds(at, width)]))
        edges = [pltpu.make_async_copy(p, q, sem.at[i]) for i, (p, q) in enumerate(edges)]
        main = [
            pltpu.make_async_copy(p, q, sem.at[len(edges) + i]) for i, (p, q) in enumerate(main)
        ]
        begin(edges)
        begin(main)
        zero = jnp.zeros((SUB, span), F32)
        for c in range(3):
            start[c, 1] = zero
            sect[c, 0] = zero
            for ref in (nb, na):
                ref[c, 0:SUB, :] = zero
                ref[c, SUB + cells :, :] = zero
        finish(edges)
        groups = cells // SUB
        edge_rows(nb, b2, b0, eb, has_before, 0, groups, span)
        edge_rows(na, a0, a2, ea, has_after, 0, groups, span)
        finish(main)
        section_plane(0, start, sect, nb, na, span)

        def body(x, _):
            section_plane(x + 1, start, sect, nb, na, span)
            second_plane(x, start, sect, eb, ea, out, span)
            pltpu.make_async_copy(out.at[:, x], out_hbm.at[:, x], out_sem.at[x]).start()
            return 0

        lax.fori_loop(0, reach, body, 0)

        def drain(x, _):
            pltpu.make_async_copy(out.at[:, x], out_hbm.at[:, x], out_sem.at[x]).wait()
            return 0

        lax.fori_loop(0, reach, drain, 0)


def call(kernel, out_shape, out_specs, in_specs, scratch, estimate, alias=None):
    def run(*args):
        return pl.pallas_call(
            kernel,
            out_shape=out_shape,
            in_specs=in_specs,
            out_specs=out_specs,
            scratch_shapes=scratch,
            input_output_aliases=alias or {},
            compiler_params=params(),
            cost_estimate=estimate,
        )(*args)

    return run


def local(velocity, noise, previous, decay, stress_factor, mean_profile):
    rows = lax.axis_size("grp")
    ranks = lax.axis_size("gx")
    comps, count, depth, span_local = noise.shape
    cells, slab, span = velocity.shape[1:]
    width = span_local // PARTS
    low = count
    high = cells - low
    dma = pltpu.SemaphoreType.DMA

    def along_gx(array, step, lines, idlers=()):
        pairs = idle(idlers) + [
            (r * ranks + i, r * ranks + i + step)
            for r in lines
            for i in range(ranks)
            if 0 <= i + step < ranks
        ]
        return lax.ppermute(array, ("grp", "gx"), pairs)

    packed = jax.ShapeDtypeStruct((comps, count, depth * HALF // LANES, LANES), F32)
    face = jax.ShapeDtypeStruct((3, 2, low, span), F32)
    face_hi = jax.ShapeDtypeStruct((3, 2, high, span), F32)
    xface = jax.ShapeDtypeStruct((3, 2, slab, span), F32)
    full = jax.ShapeDtypeStruct(velocity.shape, F32)
    rim_out, near_out, far_out = call(
        first_kernel,
        [packed, xface, xface],
        [VMEM] * 3,
        [ANY] * 2,
        [pltpu.VMEM((comps, count, depth, LANES), F32), dma((comps + 2,))],
        cost(0, noise.size),
    )(noise, velocity)

    def idle(lines):
        return [(r * ranks + i, r * ranks + (i ^ 1)) for r in lines for i in range(ranks)]

    def across(array, moves, idlers):
        pairs = [(a * ranks + i, b * ranks + i) for a, b in moves for i in range(ranks)]
        return lax.ppermute(array, ("grp", "gx"), pairs + idle(idlers))

    pairs = idle([r for r in range(rows) if r not in (1, 2)])
    for line, step in ((1, 1), (2, -1)):
        pairs += [(line * ranks + i, line * ranks + (i + step) % ranks) for i in range(ranks)]
    rim = lax.ppermute(rim_out, ("grp", "gx"), pairs)
    everyone = range(rows)
    evens = range(0, rows - 1, 2)
    odds = range(1, rows - 1, 2)
    lone = [0] + ([rows - 1] if rows % 2 == 0 else [])

    window = min(span_local, LANES * (-(-(width + 2 * HALF) // LANES) + 1))
    made_shape = jax.ShapeDtypeStruct((ranks, comps, count, depth // ranks, width), F32)

    windowed = pltpu.VMEM((comps, count, depth, window), F32)

    def make(kernel, inputs, specs, scratch):
        prev = previous
        if width % LANES:
            at = part_of(lax.axis_index("grp")) * width
            prev = lax.dynamic_slice_in_dim(previous, at, width, 2)
        return call(
            kernel,
            made_shape,
            VMEM,
            specs + [ANY, VMEM, VMEM, VMEM],
            [
                pltpu.VMEM((comps, count, depth, width), F32),
                pltpu.VMEM((comps, depth, width), F32),
            ]
            + scratch,
            cost(6 * noise.size * width, 4 * noise.size),
        )(*inputs, prev, decay, stress_factor, mean_profile[None])

    along = call(
        along_kernel,
        jax.ShapeDtypeStruct((comps, count, depth, width), F32),
        VMEM,
        [ANY],
        [windowed, dma((comps,))],
        cost(6 * noise.size * width, 4 * noise.size),
    )(noise)
    kernel_a = functools.partial(filter_kernel, span_local)
    made_a = make(
        kernel_a, [along, rim], [ANY] * 2,
        [
            pltpu.VMEM((comps, count, depth, width), F32),
            pltpu.VMEM(packed.shape, F32),
            dma((comps + 2,)),
        ],
    )
    got_a = lax.all_to_all(made_a, "gx", 0, 0, tiled=True)

    near = across(near_out, [p for i in evens for p in ((i, i + 1), (i + 1, i))], [])
    detour = []
    if rows == 4:
        far = across(far_out, [(1, 3), (2, 1)], [0])
        detour = [across(far, [(3, 2)], [0, 1])]
    else:
        far = across(far_out, [p for i in odds for p in ((i, i + 1), (i + 1, i))], lone)
    xfaces = [near, far] + detour
    face_all = jax.ShapeDtypeStruct((3, 2, cells, span), F32)
    dn_all, up_all, dn_hi, up_hi = call(
        zfaces_kernel, [face_all, face_all, face_hi, face_hi], [VMEM] * 4, [ANY] * 2,
        [dma((12,))], cost(0, velocity.size),
    )(velocity, made_a)
    others = range(1, rows)
    b_hi = along_gx(up_hi, 1, [0], others)
    a_hi = along_gx(dn_hi, -1, [0], others)

    half = ranks // 2
    side = lax.ppermute(got_a[half:], "grp", [(3, 1)])
    hop_1 = lax.ppermute(got_a, "grp", [(1, 0)])
    hop_2 = lax.ppermute(got_a, "grp", [(2, 0)])
    hop_3 = lax.ppermute(got_a[:half], "grp", [(3, 0)])

    b_all = along_gx(up_all, 1, others)
    a_all = along_gx(dn_all, -1, others)

    mark = call(
        mark_kernel, jax.ShapeDtypeStruct((SUB, LANES), F32), VMEM, [ANY], [], cost(0, 1024)
    )(made_a)
    pair = jax.ShapeDtypeStruct((3, 2, span), F32)
    up_corner, dn_corner = call(
        corners_kernel, [pair, pair], [VMEM] * 2, [ANY] * (len(xfaces) + 1), [dma((12,))],
        cost(0, 24 * span),
    )(*xfaces, mark)
    up_corners = along_gx(up_corner, 1, everyone)
    dn_corners = along_gx(dn_corner, -1, everyone)

    def fields(planes):
        return [
            pltpu.VMEM((3, planes + 4, slab, span), F32),
            pltpu.VMEM((3, planes + 2, slab, span), F32),
            pltpu.VMEM((3, planes, slab, span), F32),
        ]

    hop_4 = lax.ppermute(side, "grp", [(1, 0)])
    own = call(
        functools.partial(own_kernel, rows, ranks),
        full,
        ANY,
        [ANY] * (11 + len(xfaces)),
        fields(cells)
        + rows_scratch(cells, span)
        + [pltpu.VMEM((2, 3, 2, span), F32), dma((12,)), dma((cells,))],
        cost(50 * velocity.size, 8 * velocity.size),
    )(velocity, *xfaces, up_corners, dn_corners, dn_all, up_all, b_all, a_all, dn_hi, up_hi, b_hi,
      a_hi)

    parts = [hop_1, got_a, hop_3, hop_4, hop_2]
    places = [(0, 0, PARTS), (0, 1, PARTS), (0, 2, PARTS), (half, 2, PARTS), (0, 3, PARTS)]
    if width != LANES:
        joined = [hop_1, got_a, jnp.concatenate([hop_3, hop_4], axis=0), hop_2]
        joined = jnp.concatenate(joined, axis=4)
        parts = [joined[..., at : at + LANES] for at in range(0, span_local, LANES)]
        places = [(0, i, len(parts)) for i in range(len(parts))]
    many = len(parts)
    dn_in, up_in = call(
        functools.partial(inflow_faces_kernel, places),
        [face, face],
        [VMEM] * 2,
        [ANY] * many,
        [dma((4 * sum(p.shape[0] for p in parts),))],
        cost(0, 8 * noise.size),
    )(*parts)
    b_in = along_gx(up_in, 1, [0])
    a_in = along_gx(dn_in, -1, [0])

    reach = low + 2
    return call(
        functools.partial(inflow_kernel, rows, ranks, places),
        full,
        ANY,
        [ANY] * (many + 10),
        fields(reach)
        + rows_scratch(low + high, span)
        + [dma((sum(p.shape[0] for p in parts) + 13,)), dma((reach,))],
        cost(30 * velocity.size, 5 * velocity.size),
        {many + 9: 0},
    )(velocity, *parts, dn_in, up_in, b_in, a_in, dn_hi, up_hi, b_hi, a_hi, own)


def solution(mesh):
    placed = (
        P(None, "grp", "gx", None),
        P(None, None, None, "gx"),
        P(None, None, "gx"),
        P(),
        P(),
        P(),
    )

    return jax.shard_map(
        local, mesh=mesh, in_specs=placed, out_specs=P(None, "grp", "gx", None), check_vma=False
    )
```

```python
import functools
import math

import jax
import jax.numpy as jnp
from jax import lax
from jax.experimental import pallas as pl
from jax.experimental.pallas import tpu as pltpu
from jax.sharding import PartitionSpec as P


HALF = 32
TIME_STEP = 0.15
VISCOSITY = 0.2
LANES = 128
SUB = 8
PARTS = 4
VMEM_LIMIT = 60 * 1024 * 1024

ANY = pl.BlockSpec(memory_space=pltpu.HBM)
VMEM = pl.BlockSpec(memory_space=pltpu.VMEM)
F32 = jnp.float32


def params():
    return pltpu.CompilerParams(vmem_limit_bytes=VMEM_LIMIT)


def cost(flops, nbytes):
    return pl.CostEstimate(flops=flops, bytes_accessed=nbytes, transcendentals=0)


def kernel_norm():
    length = HALF / 2.0
    total = sum(
        math.exp(-math.pi * k * k / (2.0 * length * length)) ** 2 for k in range(-HALF, HALF + 1)
    )
    return math.sqrt(total)


def weights(offset):
    length = HALF / 2.0
    off = offset.astype(F32)
    value = jnp.exp(off * off * (-math.pi / (2.0 * length * length))) * (1.0 / kernel_norm())
    return jnp.where(jnp.abs(offset) <= HALF, value, 0.0)


def split(x):
    high = x.astype(jnp.bfloat16)
    low = (x - high.astype(F32)).astype(jnp.bfloat16)
    return high, low


def dot(a, b):
    return jnp.dot(a, b, preferred_element_type=F32)


def first_kernel(noise, vel, rim_ref, near_ref, far_ref, edge, sem):
    comps, count, depth, span = noise.shape
    groups = LANES // HALF
    rows = depth // groups
    use_left = lax.axis_index("grp") == 2
    at = pl.multiple_of(jnp.where(use_left, 0, span - LANES), LANES)
    copies = [
        pltpu.make_async_copy(noise.at[c, :, :, pl.ds(at, LANES)], edge.at[c], sem.at[c])
        for c in range(comps)
    ]
    for copy in copies:
        copy.start()
    cells = vel.shape[1]
    even = lax.rem(lax.axis_index("grp"), 2) == 0
    x = jnp.where(even, cells - 2, 0)
    faces = [
        pltpu.make_async_copy(vel.at[:, pl.ds(x, 2)], near_ref, sem.at[comps]),
        pltpu.make_async_copy(vel.at[:, pl.ds(cells - 2 - x, 2)], far_ref, sem.at[comps + 1]),
    ]
    for copy in faces:
        copy.start()
    lane = lax.broadcasted_iota(jnp.int32, (count, rows, LANES), 2)
    for c in range(comps):
        copies[c].wait()
        result = None
        for q in range(groups):
            piece = edge[c, :, rows * q : rows * (q + 1), :]
            to_left = piece if q == 0 else pltpu.roll(piece, HALF * q, 2)
            to_right = pltpu.roll(piece, (HALF * (q + 1)) % LANES, 2) if (q + 1) % groups else piece
            piece = jnp.where(use_left, to_left, to_right)
            result = piece if q == 0 else jnp.where(lane >= HALF * q, piece, result)
        rim_ref[c] = result
    for copy in faces:
        copy.wait()


def face_copies(vel, first, cells, dn, up, sem, at):
    slab = vel.shape[2]
    copies = []
    for c in range(3):
        for j in range(2):
            for ref, z in ((dn, j), (up, slab - 2 + j)):
                copies.append(
                    pltpu.make_async_copy(
                        vel.at[c, pl.ds(first, cells), z], ref.at[c, j], sem.at[at + len(copies)]
                    )
                )
    return copies


def zfaces_kernel(vel, after, all_dn, all_up, high_dn, high_up, sem):
    del after
    cells, high = all_dn.shape[2], high_dn.shape[2]
    is_first = lax.axis_index("grp") == 0

    @pl.when(is_first)
    def _():
        run_copies(face_copies(vel, cells - high, high, high_dn, high_up, sem, 0))

    @pl.when(jnp.logical_not(is_first))
    def _():
        run_copies(face_copies(vel, 0, cells, all_dn, all_up, sem, 0))


def mark_kernel(after, out_ref):
    del after
    out_ref[...] = jnp.zeros_like(out_ref)


def column(ref, c, width):
    depth = ref.shape[1]
    row = lax.broadcasted_iota(jnp.int32, (depth, depth), 0)
    col = lax.broadcasted_iota(jnp.int32, (depth, depth), 1)
    value = jnp.where(row == col, jnp.broadcast_to(ref[c : c + 1, :], (depth, depth)), 0.0)
    return jnp.broadcast_to(jnp.sum(value, axis=1, keepdims=True), (depth, width))


def part_of(line):
    return jnp.where(line == 0, 1, jnp.where(line == 1, 0, jnp.where(line == 2, PARTS - 1, 2)))


def window_of(line, width, whole, span):
    first = part_of(line) * width
    start = jnp.minimum(jnp.maximum((first - HALF) // LANES * LANES, 0), whole - span)
    return first, pl.multiple_of(start, LANES)


def spanwise_band(base, span, width):
    row = lax.broadcasted_iota(jnp.int32, (span, width), 0)
    col = lax.broadcasted_iota(jnp.int32, (span, width), 1)
    high, low = split(weights(row - col - base))
    return jnp.concatenate([high, high, low], axis=0)


def window_copies(noise, noise_ref, start, sem):
    comps, _, _, span = noise_ref.shape
    return [
        pltpu.make_async_copy(noise.at[c, :, :, pl.ds(start, span)], noise_ref.at[c], sem.at[c])
        for c in range(comps)
    ]


def along_kernel(noise, out_ref, noise_ref, sem):
    comps, count, depth, span = noise_ref.shape
    width = out_ref.shape[3]
    line = lax.axis_index("grp")
    first, start = window_of(line, width, noise.shape[3], span)
    copies = window_copies(noise, noise_ref, start, sem)
    for copy in copies:
        copy.start()
    band = spanwise_band(first - start, span, width)
    for c in range(comps):
        copies[c].wait()
        high, low = split(noise_ref[c].reshape(count * depth, span))
        along = dot(jnp.concatenate([high, low, high], axis=1), band)
        out_ref[c] = along.reshape(count, depth, width)


def filter_kernel(whole, along_hbm, rim, previous, decay_ref, factor_ref, mean_ref,
                    out_ref, planes_ref, prev_ref, along_ref, rim_ref, sem):
    comps, count, depth, width = along_ref.shape
    line = lax.axis_index("grp")
    first = part_of(line) * width
    before = previous_copy(previous, prev_ref, first, sem.at[0])
    rim_copy = pltpu.make_async_copy(rim, rim_ref, sem.at[1])
    along_copies = [
        pltpu.make_async_copy(along_hbm.at[c], along_ref.at[c], sem.at[2 + c])
        for c in range(comps)
    ]
    for copy in [rim_copy, before] + along_copies:
        copy.start()
    groups = LANES // HALF
    rows = depth // groups
    rim_at = jnp.where(line == 2, whole, -HALF) - first
    hrow = lax.broadcasted_iota(jnp.int32, (LANES, width), 0)
    hcol = lax.broadcasted_iota(jnp.int32, (LANES, width), 1)
    bands = []
    for q in range(groups):
        cell = hrow - HALF * q
        value = weights(cell + rim_at - hcol)
        high, low = split(jnp.where((cell >= 0) & (cell < HALF), value, 0.0))
        bands.append(jnp.concatenate([high, high, low], axis=0))
    band = jnp.concatenate(bands, axis=1)

    rim_copy.wait()

    def along(c):
        along_copies[c].wait()
        high, low = split(rim_ref[c].reshape(count * rows, LANES))
        part = dot(jnp.concatenate([high, low, high], axis=1), band)
        part = part.reshape(count, rows, groups * width)
        extra = [part[:, :, width * q : width * (q + 1)] for q in range(groups)]
        return along_ref[c] + jnp.concatenate(extra, axis=1)

    inflow_planes(along, before, decay_ref, factor_ref, mean_ref, out_ref, planes_ref, prev_ref)


def previous_copy(previous, prev_ref, first, sem):
    width = prev_ref.shape[2]
    if width % LANES == 0:
        previous = previous.at[:, :, pl.ds(pl.multiple_of(first, LANES), width)]
    return pltpu.make_async_copy(previous, prev_ref, sem)


def inflow_planes(along, before, decay_ref, factor_ref, mean_ref, out_ref, planes_ref, prev_ref):
    comps, count, depth, width = planes_ref.shape
    zrow = lax.broadcasted_iota(jnp.int32, (depth, depth), 0)
    zcol = lax.broadcasted_iota(jnp.int32, (depth, depth), 1)
    zh, zl = split(weights(zrow - zcol))
    zband = jnp.concatenate([zh, zh, zl], axis=1)
    for c in range(comps):
        value = along(c)
        wide = jnp.concatenate([value[p] for p in range(count)], axis=1)
        yh, yl = split(wide)
        smooth = dot(zband, jnp.concatenate([yh, yl, yh], axis=0))
        if c == 0:
            before.wait()
        dec = column(decay_ref, c, width)
        scale = jnp.sqrt(1.0 - dec * dec)
        carried = prev_ref[c]
        for p in range(count):
            carried = dec * carried + scale * smooth[:, p * width : (p + 1) * width]
            planes_ref[c, p] = carried
    owners = out_ref.shape[0]
    slab = depth // owners

    def put(c, p, value):
        for d in range(owners):
            out_ref[d, c, p] = value[slab * d : slab * (d + 1)]

    mean = column(mean_ref, 0, width)
    factor = [column(factor_ref, i, width) for i in range(6)]
    for p in range(count):
        a, b, d = planes_ref[0, p], planes_ref[1, p], planes_ref[2, p]
        put(0, p, mean + factor[0] * a)
        put(1, p, factor[1] * a + factor[2] * b)
        put(2, p, factor[3] * a + factor[4] * b + factor[5] * d)


def sides(near, far, detour):
    line = lax.axis_index("grp")
    even = lax.rem(line, 2) == 0
    odd = (jnp.logical_not(even), near, far)
    if detour is None:
        return [(even, far, near), odd]
    return [(line == 2, detour, near), (jnp.logical_and(even, line != 2), far, near), odd]


def corners_kernel(*refs):
    near, far, *detour, _, up_ref, dn_ref, sem = refs
    slab = near.shape[2]

    def rows(left, right):
        copies = []
        for ref, z in ((up_ref, slab - 1), (dn_ref, 0)):
            for i, (face, x) in enumerate(((left, 1), (right, 0))):
                for c in range(3):
                    copies.append(
                        pltpu.make_async_copy(face.at[c, x, z], ref.at[c, i], sem.at[len(copies)])
                    )
        return copies

    for condition, left, right in sides(near, far, detour[0] if detour else None):

        @pl.when(condition)
        def _(left=left, right=right):
            run_copies(rows(left, right))


def inflow_faces_kernel(*refs):
    pieces = refs[:-3]
    dn, up, sem = refs[-3:]
    copies, first = [], 0
    for piece in pieces:
        count, slab = piece.shape[0], piece.shape[3]
        for j in range(2):
            for ref, z in ((dn, j), (up, slab - 2 + j)):
                copies.append(
                    pltpu.make_async_copy(
                        piece.at[:, :, :, z],
                        ref.at[pl.ds(first, count), :, j],
                        sem.at[len(copies)],
                    )
                )
        first += count

    @pl.when(lax.axis_index("grp") == 0)
    def _():
        run_copies(copies)


A = VISCOSITY * TIME_STEP
H = 0.5 * TIME_STEP
B = 1.0 - 6.0 * A
BLOCK = 512


def combine(scale, cs, xp, xn, zp, zn, yp, yn):
    a, h, b = A * scale, H * scale, B * scale
    cu, cw, cv = h * cs[0], h * cs[1], h * cs[2]
    out = []
    for i in range(3):
        total = xn[i] * (a - cu) + xp[i] * (a + cu)
        total = total + (zn[i] * (a - cw) + zp[i] * (a + cw))
        total = total + (yn[i] * (a - cv) + yp[i] * (a + cv))
        out.append(total + b * cs[i])
    return out


def spanwise(load, at, width, span):
    centre = load(at, width)
    wide = jnp.concatenate(
        [load((at - LANES) % span, LANES), centre, load((at + width) % span, LANES)], axis=1
    )
    total = width + 2 * LANES
    before = pltpu.roll(wide, 1, 1)[:, LANES : LANES + width]
    after = pltpu.roll(wide, total - 1, 1)[:, LANES : LANES + width]
    return centre, before, after


def main_block(scale, field, x, zb, za, zrow, at, width, span):
    top = lax.broadcasted_iota(jnp.int32, (SUB, width), 0)
    cs, xp, xn, zp, zn, yp, yn = [], [], [], [], [], [], []
    for c in range(3):
        centre, before, after = spanwise(
            lambda l, w, c=c: field[c, x, :, pl.ds(l, w)], at, width, span
        )
        cs.append(centre)
        yp.append(before)
        yn.append(after)
        xp.append(field[c, x - 1, :, pl.ds(at, width)])
        xn.append(field[c, x + 1, :, pl.ds(at, width)])
        low = jnp.broadcast_to(zb[c, pl.ds(zrow, 1), pl.ds(at, width)], (SUB, width))
        high = jnp.broadcast_to(za[c, pl.ds(zrow, 1), pl.ds(at, width)], (SUB, width))
        zp.append(jnp.where(top == 0, low, pltpu.roll(centre, 1, 0)))
        zn.append(jnp.where(top == SUB - 1, high, pltpu.roll(centre, SUB - 1, 0)))
    return combine(scale, cs, xp, xn, zp, zn, yp, yn)


def edge_rows(near, before, after, out, keep, begin, groups, span):
    def block(i, _):
        at = pl.multiple_of(i * BLOCK, BLOCK)
        left = pl.multiple_of(lax.rem(at + span - LANES, span), LANES)
        right = pl.multiple_of(lax.rem(at + BLOCK, span), LANES)
        for g in range(begin, groups):
            cs, xp, xn, zp, zn, yp, yn = [], [], [], [], [], [], []
            for c in range(3):
                r = SUB * (g + 1)
                centre = near[c, r : r + SUB, pl.ds(at, BLOCK)]
                wide = jnp.concatenate(
                    [
                        near[c, r : r + SUB, pl.ds(left, LANES)],
                        centre,
                        near[c, r : r + SUB, pl.ds(right, LANES)],
                    ],
                    axis=1,
                )
                total = BLOCK + 2 * LANES
                cs.append(centre)
                yp.append(pltpu.roll(wide, 1, 1)[:, LANES : LANES + BLOCK])
                yn.append(pltpu.roll(wide, total - 1, 1)[:, LANES : LANES + BLOCK])
                xp.append(near[c, r - 1 : r - 1 + SUB, pl.ds(at, BLOCK)])
                xn.append(near[c, r + 1 : r + 1 + SUB, pl.ds(at, BLOCK)])
                zp.append(before[c, SUB * g : SUB * (g + 1), pl.ds(at, BLOCK)])
                zn.append(after[c, SUB * g : SUB * (g + 1), pl.ds(at, BLOCK)])
            new = combine(1.0, cs, xp, xn, zp, zn, yp, yn)
            for c in range(3):
                out[c, SUB * (g + 1) : SUB * (g + 2), pl.ds(at, BLOCK)] = jnp.where(
                    keep, new[c], 0.0
                )
        return 0

    lax.fori_loop(0, span // BLOCK, block, 0)


def section_plane(x, start, sect, nb, na, span, keep=None):
    for at in range(0, span, BLOCK):
        new = main_block(1.0, start, x + 2, nb, na, SUB + x, at, BLOCK, span)
        for c in range(3):
            value = new[c] if keep is None else jnp.where(keep, new[c], 0.0)
            sect[c, x + 1, :, at : at + BLOCK] = value


def second_plane(x, start, sect, eb, ea, out, span):
    for at in range(0, span, BLOCK):
        new = main_block(0.5, sect, x + 1, eb, ea, SUB + x, at, BLOCK, span)
        for c in range(3):
            out[c, x, :, at : at + BLOCK] = new[c] + 0.5 * start[c, x + 2, :, at : at + BLOCK]


def rows_scratch(cells, span):
    shift = [
        pltpu.VMEM((3, cells + 2 * SUB, span), F32),
        pltpu.VMEM((3, cells + 2 * SUB, span), F32),
    ]
    side = [pltpu.VMEM((3, cells, span), F32)] * 4
    return shift + side + shift


def begin(copies, condition=None):
    if condition is not None:
        pl.when(condition)(lambda: begin(copies))
        return
    for copy in copies:
        copy.start()


def finish(copies, condition=None):
    if condition is not None:
        pl.when(condition)(lambda: finish(copies))
        return
    for copy in copies:
        copy.wait()


def run_copies(copies):
    for copy in copies:
        copy.start()
    for copy in copies:
        copy.wait()


def roles(rows, ranks):
    r, g = lax.axis_index("grp"), lax.axis_index("gx")
    return g > 0, g < ranks - 1, r > 0, r < rows - 1, r == 0


ROWS = ((2, 1, 0, SUB), (3, 0, 1, SUB), (2, 0, 2, 0), (0, 0, 3, 0), (1, 1, 4, 0), (3, 1, 5, 0))


def row_pieces(faces, first, *scratch):
    count = faces[0].shape[2]
    return [
        (faces[i].at[:, j], scratch[ref].at[:, pl.ds(at + first, count)])
        for i, j, ref, at in ROWS
    ]


def own_kernel(rows, ranks, vel, *refs):
    near, far, *detour = refs[:-25]
    (up_corners, dn_corners, dn_all, up_all, b_all, a_all, dn_hi, up_hi, b_hi, a_hi, out_hbm,
     start, sect, out, nb, na, b2, b0, a0, a2, eb, ea, corner, sem, out_sem) = refs[-25:]
    cells = vel.shape[1]
    low = cells - dn_hi.shape[2]
    span = vel.shape[3]
    has_before, has_after, has_left, has_right, is_first = roles(rows, ranks)
    first = jnp.where(is_first, low + 2, 0)
    is_other = jnp.logical_not(is_first)
    left_at, right_at = start.at[:, pl.ds(0, 2)], start.at[:, pl.ds(cells + 2, 2)]
    rows_first = row_pieces((dn_hi, up_hi, b_hi, a_hi), low, nb, na, b2, b0, a0, a2)
    rows_other = row_pieces((dn_all, up_all, b_all, a_all), 0, nb, na, b2, b0, a0, a2)
    ends = [(up_corners, corner.at[0]), (dn_corners, corner.at[1])]
    main = [(vel.at[:, pl.ds(low, cells - low)], start.at[:, pl.ds(2 + low, cells - low)])]
    rest = [(vel.at[:, pl.ds(0, low)], start.at[:, pl.ds(2, low)])]

    def copies(pieces, at):
        return [pltpu.make_async_copy(p, q, sem.at[at + i]) for i, (p, q) in enumerate(pieces)]

    begin(copies(rows_first, 0), is_first)
    begin(copies(rows_other, 0), is_other)
    begin(copies(ends, 6))
    begin(copies(main, 8))
    for condition, left, right in sides(near, far, detour[0] if detour else None):
        begin(copies([(right, right_at)], 9), condition)
        begin(copies([(left, left_at)], 10), jnp.logical_and(condition, is_other))
    begin(copies(rest, 11), is_other)
    finish(copies(rows_first, 0), is_first)
    finish(copies(rows_other, 0), is_other)
    finish(copies(ends, 6))

    @pl.when(jnp.logical_not(has_right))
    def _():
        for c in range(3):
            for i in range(2):
                corner[i, c, 1:2, :] = jnp.zeros((1, span), F32)

    for c in range(3):
        nb[c, SUB - 1 : SUB, :] = corner[0, c, 0:1, :]
        nb[c, SUB + cells : SUB + cells + 1, :] = corner[0, c, 1:2, :]
        na[c, SUB - 1 : SUB, :] = corner[1, c, 0:1, :]
        na[c, SUB + cells : SUB + cells + 1, :] = corner[1, c, 1:2, :]
    groups = cells // SUB

    @pl.when(jnp.logical_not(is_first))
    def _():
        edge_rows(nb, b2, b0, eb, has_before, 0, low // SUB, span)
        edge_rows(na, a0, a2, ea, has_after, 0, low // SUB, span)

    edge_rows(nb, b2, b0, eb, has_before, low // SUB, groups, span)
    edge_rows(na, a0, a2, ea, has_after, low // SUB, groups, span)
    finish(copies(main, 8))
    finish(copies([(near, right_at)], 9))
    finish(copies([(near, left_at)], 10), is_other)
    finish(copies(rest, 11), is_other)

    @pl.when(jnp.logical_not(has_right))
    def _():
        for c in range(3):
            start[c, cells + 2] = jnp.zeros((SUB, span), F32)

    def make(x, keep=None):
        section_plane(x, start, sect, nb, na, span, keep)

    def body(x, _):
        keep = jnp.logical_or(
            jnp.logical_and(x >= 0, x < cells),
            jnp.logical_or(jnp.logical_and(x < 0, has_left), jnp.logical_and(x >= cells, has_right)),
        )
        make(x, keep)

        @pl.when(x >= first + 1)
        def _():
            second_plane(x - 1, start, sect, eb, ea, out, span)
            pltpu.make_async_copy(out.at[:, x - 1], out_hbm.at[:, x - 1], out_sem.at[x - 1]).start()

        return 0

    lax.fori_loop(first - 1, cells + 1, body, 0)

    def drain(x, _):
        pltpu.make_async_copy(out.at[:, x], out_hbm.at[:, x], out_sem.at[x]).wait()
        return 0

    lax.fori_loop(first, cells, drain, 0)


def inflow_kernel(rows, ranks, groups_of, vel, *refs):
    many = sum(len(places) for places in groups_of)
    parts, refs = refs[:many], refs[many:]
    faces, refs = refs[: 4 * len(groups_of)], refs[4 * len(groups_of) :]
    dn_hi, up_hi, b_hi, a_hi, _, out_hbm = refs[:6]
    start, sect, out, nb, na, b2, b0, a0, a2, eb, ea, spread, sem, out_sem = refs[6:]
    cells = b2.shape[1]
    low = cells - dn_hi.shape[2]
    span = vel.shape[3]
    reach = out.shape[1]
    has_before, has_after, _, _, is_first = roles(rows, ranks)
    scratch = (nb, na, b2, b0, a0, a2)

    @pl.when(is_first)
    def _():
        edges = row_pieces((dn_hi, up_hi, b_hi, a_hi), low, *scratch)
        main = [(vel.at[:, pl.ds(low, 4)], start.at[:, pl.ds(low + 2, 4)])]
        lanes_of, at = [], 0
        for k, places in enumerate(groups_of):
            first = len(lanes_of)
            for piece, (source, part, parts_in) in zip(parts[at : at + len(places)], places):
                width = piece.shape[4]
                for i in range(piece.shape[0]):
                    lane = ((source + i) * parts_in + part) * width
                    main.append((piece.at[i], start.at[:, pl.ds(2, low), :, pl.ds(lane, width)]))
                    lanes_of.append(lane)
            at += len(places)
            for i in range(4):
                face = faces[4 * k + i]
                edges.append((face, spread.at[i, pl.ds(first, len(lanes_of) - first)]))
        edges = [pltpu.make_async_copy(p, q, sem.at[i]) for i, (p, q) in enumerate(edges)]
        main = [
            pltpu.make_async_copy(p, q, sem.at[len(edges) + i]) for i, (p, q) in enumerate(main)
        ]
        begin(edges)
        begin(main)
        zero = jnp.zeros((SUB, span), F32)
        for c in range(3):
            start[c, 1] = zero
            sect[c, 0] = zero
            for ref in (nb, na):
                ref[c, 0:SUB, :] = zero
                ref[c, SUB + cells :, :] = zero
        finish(edges)
        for n, lane in enumerate(lanes_of):
            for i, j, ref, first in ROWS:
                for c in range(3):
                    scratch[ref][c, first : first + low, lane : lane + LANES] = spread[i, n, c, j]
        groups = cells // SUB
        edge_rows(nb, b2, b0, eb, has_before, 0, groups, span)
        edge_rows(na, a0, a2, ea, has_after, 0, groups, span)
        finish(main)
        section_plane(0, start, sect, nb, na, span)

        def body(x, _):
            section_plane(x + 1, start, sect, nb, na, span)
            second_plane(x, start, sect, eb, ea, out, span)
            pltpu.make_async_copy(out.at[:, x], out_hbm.at[:, x], out_sem.at[x]).start()
            return 0

        lax.fori_loop(0, reach, body, 0)

        def drain(x, _):
            pltpu.make_async_copy(out.at[:, x], out_hbm.at[:, x], out_sem.at[x]).wait()
            return 0

        lax.fori_loop(0, reach, drain, 0)


def call(kernel, out_shape, out_specs, in_specs, scratch, estimate, alias=None):
    def run(*args):
        return pl.pallas_call(
            kernel,
            out_shape=out_shape,
            in_specs=in_specs,
            out_specs=out_specs,
            scratch_shapes=scratch,
            input_output_aliases=alias or {},
            compiler_params=params(),
            cost_estimate=estimate,
        )(*args)

    return run


def local(velocity, noise, previous, decay, stress_factor, mean_profile):
    rows = lax.axis_size("grp")
    ranks = lax.axis_size("gx")
    comps, count, depth, span_local = noise.shape
    cells, slab, span = velocity.shape[1:]
    width = span_local // PARTS
    low = count
    high = cells - low
    dma = pltpu.SemaphoreType.DMA

    def along_gx(array, step, lines, idlers=()):
        pairs = idle(idlers) + [
            (r * ranks + i, r * ranks + i + step)
            for r in lines
            for i in range(ranks)
            if 0 <= i + step < ranks
        ]
        return lax.ppermute(array, ("grp", "gx"), pairs)

    packed = jax.ShapeDtypeStruct((comps, count, depth * HALF // LANES, LANES), F32)
    face_hi = jax.ShapeDtypeStruct((3, 2, high, span), F32)
    xface = jax.ShapeDtypeStruct((3, 2, slab, span), F32)
    full = jax.ShapeDtypeStruct(velocity.shape, F32)
    rim_out, near_out, far_out = call(
        first_kernel,
        [packed, xface, xface],
        [VMEM] * 3,
        [ANY] * 2,
        [pltpu.VMEM((comps, count, depth, LANES), F32), dma((comps + 2,))],
        cost(0, noise.size),
    )(noise, velocity)

    def idle(lines):
        return [(r * ranks + i, r * ranks + (i ^ 1)) for r in lines for i in range(ranks)]

    def across(array, moves, idlers):
        pairs = [(a * ranks + i, b * ranks + i) for a, b in moves for i in range(ranks)]
        return lax.ppermute(array, ("grp", "gx"), pairs + idle(idlers))

    pairs = idle([r for r in range(rows) if r not in (1, 2)])
    for line, step in ((1, 1), (2, -1)):
        pairs += [(line * ranks + i, line * ranks + (i + step) % ranks) for i in range(ranks)]
    rim = lax.ppermute(rim_out, ("grp", "gx"), pairs)
    everyone = range(rows)
    evens = range(0, rows - 1, 2)
    odds = range(1, rows - 1, 2)
    lone = [0] + ([rows - 1] if rows % 2 == 0 else [])

    window = min(span_local, LANES * (-(-(width + 2 * HALF) // LANES) + 1))
    made_shape = jax.ShapeDtypeStruct((ranks, comps, count, depth // ranks, width), F32)

    windowed = pltpu.VMEM((comps, count, depth, window), F32)

    def make(kernel, inputs, specs, scratch):
        prev = previous
        if width % LANES:
            at = part_of(lax.axis_index("grp")) * width
            prev = lax.dynamic_slice_in_dim(previous, at, width, 2)
        return call(
            kernel,
            made_shape,
            VMEM,
            specs + [ANY, VMEM, VMEM, VMEM],
            [
                pltpu.VMEM((comps, count, depth, width), F32),
                pltpu.VMEM((comps, depth, width), F32),
            ]
            + scratch,
            cost(6 * noise.size * width, 4 * noise.size),
        )(*inputs, prev, decay, stress_factor, mean_profile[None])

    along = call(
        along_kernel,
        jax.ShapeDtypeStruct((comps, count, depth, width), F32),
        VMEM,
        [ANY],
        [windowed, dma((comps,))],
        cost(6 * noise.size * width, 4 * noise.size),
    )(noise)
    kernel_a = functools.partial(filter_kernel, span_local)
    made_a = make(
        kernel_a, [along, rim], [ANY] * 2,
        [
            pltpu.VMEM((comps, count, depth, width), F32),
            pltpu.VMEM(packed.shape, F32),
            dma((comps + 2,)),
        ],
    )
    got_a = lax.all_to_all(made_a, "gx", 0, 0, tiled=True)

    near = across(near_out, [p for i in evens for p in ((i, i + 1), (i + 1, i))], [])
    detour = []
    if rows == 4:
        far = across(far_out, [(1, 3), (2, 1)], [0])
        detour = [across(far, [(3, 2)], [0, 1])]
    else:
        far = across(far_out, [p for i in odds for p in ((i, i + 1), (i + 1, i))], lone)
    xfaces = [near, far] + detour
    face_all = jax.ShapeDtypeStruct((3, 2, cells, span), F32)
    dn_all, up_all, dn_hi, up_hi = call(
        zfaces_kernel, [face_all, face_all, face_hi, face_hi], [VMEM] * 4, [ANY] * 2,
        [dma((12,))], cost(0, velocity.size),
    )(velocity, made_a)
    others = range(1, rows)
    b_hi = along_gx(up_hi, 1, [0], others)
    a_hi = along_gx(dn_hi, -1, [0], others)

    half = ranks // 2
    side = lax.ppermute(got_a[half:], "grp", [(3, 1)])
    hop_1 = lax.ppermute(got_a, "grp", [(1, 0)])
    hop_2 = lax.ppermute(got_a, "grp", [(2, 0)])
    hop_3 = lax.ppermute(got_a[:half], "grp", [(3, 0)])

    b_all = along_gx(up_all, 1, others)
    a_all = along_gx(dn_all, -1, others)

    mark = call(
        mark_kernel, jax.ShapeDtypeStruct((SUB, LANES), F32), VMEM, [ANY], [], cost(0, 1024)
    )(made_a)
    pair = jax.ShapeDtypeStruct((3, 2, span), F32)
    up_corner, dn_corner = call(
        corners_kernel, [pair, pair], [VMEM] * 2, [ANY] * (len(xfaces) + 1), [dma((12,))],
        cost(0, 24 * span),
    )(*xfaces, mark)
    up_corners = along_gx(up_corner, 1, everyone)
    dn_corners = along_gx(dn_corner, -1, everyone)

    def fields(planes):
        return [
            pltpu.VMEM((3, planes + 4, slab, span), F32),
            pltpu.VMEM((3, planes + 2, slab, span), F32),
            pltpu.VMEM((3, planes, slab, span), F32),
        ]

    hop_4 = lax.ppermute(side, "grp", [(1, 0)])
    own = call(
        functools.partial(own_kernel, rows, ranks),
        full,
        ANY,
        [ANY] * (11 + len(xfaces)),
        fields(cells)
        + rows_scratch(cells, span)
        + [pltpu.VMEM((2, 3, 2, span), F32), dma((12,)), dma((cells,))],
        cost(50 * velocity.size, 8 * velocity.size),
    )(velocity, *xfaces, up_corners, dn_corners, dn_all, up_all, b_all, a_all, dn_hi, up_hi, b_hi,
      a_hi)

    parts = [[hop_1, got_a, hop_3, hop_4, hop_2]]
    groups_of = [
        [(0, 0, PARTS), (0, 1, PARTS), (0, 2, PARTS), (half, 2, PARTS), (0, 3, PARTS)]
    ]
    if width != LANES:
        joined = [hop_1, got_a, jnp.concatenate([hop_3, hop_4], axis=0), hop_2]
        joined = jnp.concatenate(joined, axis=4)
        parts = [[joined[..., at : at + LANES] for at in range(0, span_local, LANES)]]
        groups_of = [[(0, i, len(parts[0])) for i in range(len(parts[0]))]]
    faces = []
    for group in parts:
        number = sum(p.shape[0] for p in group)
        part_face = jax.ShapeDtypeStruct((number, 3, 2, low, LANES), F32)
        dn_in, up_in = call(
            inflow_faces_kernel,
            [part_face, part_face],
            [VMEM] * 2,
            [ANY] * len(group),
            [dma((4 * len(group),))],
            cost(0, 2 * noise.size),
        )(*group)
        b_in = along_gx(up_in, 1, [0])
        a_in = along_gx(dn_in, -1, [0])
        faces += [dn_in, up_in, b_in, a_in]
    parts = [p for group in parts for p in group]
    many = len(parts) + len(faces)
    number = sum(p.shape[0] for p in parts)

    reach = low + 2
    return call(
        functools.partial(inflow_kernel, rows, ranks, groups_of),
        full,
        ANY,
        [ANY] * (many + 6),
        fields(reach)
        + rows_scratch(low + high, span)
        + [
            pltpu.VMEM((4, number, 3, 2, low, LANES), F32),
            dma((number + 7 + len(faces),)),
            dma((reach,)),
        ],
        cost(30 * velocity.size, 5 * velocity.size),
        {many + 5: 0},
    )(velocity, *parts, *faces, dn_hi, up_hi, b_hi, a_hi, own)


def solution(mesh):
    placed = (
        P(None, "grp", "gx", None),
        P(None, None, None, "gx"),
        P(None, None, "gx"),
        P(),
        P(),
        P(),
    )

    return jax.shard_map(
        local, mesh=mesh, in_specs=placed, out_specs=P(None, "grp", "gx", None), check_vma=False
    )
```

```python
import functools
import math

import jax
import jax.numpy as jnp
from jax import lax
from jax.experimental import pallas as pl
from jax.experimental.pallas import tpu as pltpu
from jax.sharding import PartitionSpec as P


HALF = 32
TIME_STEP = 0.15
VISCOSITY = 0.2
LANES = 128
SUB = 8
PARTS = 4
VMEM_LIMIT = 60 * 1024 * 1024

ANY = pl.BlockSpec(memory_space=pltpu.HBM)
VMEM = pl.BlockSpec(memory_space=pltpu.VMEM)
F32 = jnp.float32


def params():
    return pltpu.CompilerParams(vmem_limit_bytes=VMEM_LIMIT)


def cost(flops, nbytes):
    return pl.CostEstimate(flops=flops, bytes_accessed=nbytes, transcendentals=0)


def kernel_norm():
    length = HALF / 2.0
    total = sum(
        math.exp(-math.pi * k * k / (2.0 * length * length)) ** 2 for k in range(-HALF, HALF + 1)
    )
    return math.sqrt(total)


def weights(offset):
    length = HALF / 2.0
    off = offset.astype(F32)
    value = jnp.exp(off * off * (-math.pi / (2.0 * length * length))) * (1.0 / kernel_norm())
    return jnp.where(jnp.abs(offset) <= HALF, value, 0.0)


def split(x):
    high = x.astype(jnp.bfloat16)
    low = (x - high.astype(F32)).astype(jnp.bfloat16)
    return high, low


def dot(a, b):
    return jnp.dot(a, b, preferred_element_type=F32)


def first_kernel(noise, vel, rim_ref, near_ref, far_ref, edge, sem):
    comps, count, depth, span = noise.shape
    groups = LANES // HALF
    rows = depth // groups
    use_left = lax.axis_index("grp") == 2
    at = pl.multiple_of(jnp.where(use_left, 0, span - LANES), LANES)
    copies = [
        pltpu.make_async_copy(noise.at[c, :, :, pl.ds(at, LANES)], edge.at[c], sem.at[c])
        for c in range(comps)
    ]
    for copy in copies:
        copy.start()
    cells = vel.shape[1]
    even = lax.rem(lax.axis_index("grp"), 2) == 0
    x = jnp.where(even, cells - 2, 0)
    faces = [
        pltpu.make_async_copy(vel.at[:, pl.ds(x, 2)], near_ref, sem.at[comps]),
        pltpu.make_async_copy(vel.at[:, pl.ds(cells - 2 - x, 2)], far_ref, sem.at[comps + 1]),
    ]
    for copy in faces:
        copy.start()
    lane = lax.broadcasted_iota(jnp.int32, (count, rows, LANES), 2)
    for c in range(comps):
        copies[c].wait()
        result = None
        for q in range(groups):
            piece = edge[c, :, rows * q : rows * (q + 1), :]
            to_left = piece if q == 0 else pltpu.roll(piece, HALF * q, 2)
            to_right = pltpu.roll(piece, (HALF * (q + 1)) % LANES, 2) if (q + 1) % groups else piece
            piece = jnp.where(use_left, to_left, to_right)
            result = piece if q == 0 else jnp.where(lane >= HALF * q, piece, result)
        rim_ref[c] = result
    for copy in faces:
        copy.wait()


def face_copies(vel, first, cells, dn, up, sem, at):
    slab = vel.shape[2]
    copies = []
    for c in range(3):
        for j in range(2):
            for ref, z in ((dn, j), (up, slab - 2 + j)):
                copies.append(
                    pltpu.make_async_copy(
                        vel.at[c, pl.ds(first, cells), z], ref.at[c, j], sem.at[at + len(copies)]
                    )
                )
    return copies


def zfaces_kernel(vel, after, all_dn, all_up, high_dn, high_up, sem):
    del after
    cells, high = all_dn.shape[2], high_dn.shape[2]
    is_first = lax.axis_index("grp") == 0

    @pl.when(is_first)
    def _():
        run_copies(face_copies(vel, cells - high, high, high_dn, high_up, sem, 0))

    @pl.when(jnp.logical_not(is_first))
    def _():
        run_copies(face_copies(vel, 0, cells, all_dn, all_up, sem, 0))


def mark_kernel(after, out_ref):
    del after
    out_ref[...] = jnp.zeros_like(out_ref)


def column(ref, c, width):
    depth = ref.shape[1]
    row = lax.broadcasted_iota(jnp.int32, (depth, depth), 0)
    col = lax.broadcasted_iota(jnp.int32, (depth, depth), 1)
    value = jnp.where(row == col, jnp.broadcast_to(ref[c : c + 1, :], (depth, depth)), 0.0)
    return jnp.broadcast_to(jnp.sum(value, axis=1, keepdims=True), (depth, width))


def part_of(line):
    return jnp.where(line == 0, 1, jnp.where(line == 1, 0, jnp.where(line == 2, PARTS - 1, 2)))


def window_of(line, width, whole, span):
    first = part_of(line) * width
    start = jnp.minimum(jnp.maximum((first - HALF) // LANES * LANES, 0), whole - span)
    return first, pl.multiple_of(start, LANES)


def spanwise_band(base, span, width):
    row = lax.broadcasted_iota(jnp.int32, (span, width), 0)
    col = lax.broadcasted_iota(jnp.int32, (span, width), 1)
    high, low = split(weights(row - col - base))
    return jnp.concatenate([high, high, low], axis=0)


def window_copies(noise, noise_ref, start, sem):
    comps, _, _, span = noise_ref.shape
    return [
        pltpu.make_async_copy(noise.at[c, :, :, pl.ds(start, span)], noise_ref.at[c], sem.at[c])
        for c in range(comps)
    ]


def along_kernel(noise, out_ref, noise_ref, sem):
    comps, count, depth, span = noise_ref.shape
    width = out_ref.shape[3]
    line = lax.axis_index("grp")
    first, start = window_of(line, width, noise.shape[3], span)
    copies = window_copies(noise, noise_ref, start, sem)
    for copy in copies:
        copy.start()
    band = spanwise_band(first - start, span, width)
    for c in range(comps):
        copies[c].wait()
        high, low = split(noise_ref[c].reshape(count * depth, span))
        along = dot(jnp.concatenate([high, low, high], axis=1), band)
        out_ref[c] = along.reshape(count, depth, width)


def filter_kernel(whole, along_hbm, rim, previous, decay_ref, factor_ref, mean_ref,
                    out_ref, planes_ref, prev_ref, along_ref, rim_ref, sem):
    comps, count, depth, width = along_ref.shape
    line = lax.axis_index("grp")
    first = part_of(line) * width
    before = previous_copy(previous, prev_ref, first, sem.at[0])
    rim_copy = pltpu.make_async_copy(rim, rim_ref, sem.at[1])
    along_copies = [
        pltpu.make_async_copy(along_hbm.at[c], along_ref.at[c], sem.at[2 + c])
        for c in range(comps)
    ]
    for copy in [rim_copy, before] + along_copies:
        copy.start()
    groups = LANES // HALF
    rows = depth // groups
    rim_at = jnp.where(line == 2, whole, -HALF) - first
    hrow = lax.broadcasted_iota(jnp.int32, (LANES, width), 0)
    hcol = lax.broadcasted_iota(jnp.int32, (LANES, width), 1)
    bands = []
    for q in range(groups):
        cell = hrow - HALF * q
        value = weights(cell + rim_at - hcol)
        high, low = split(jnp.where((cell >= 0) & (cell < HALF), value, 0.0))
        bands.append(jnp.concatenate([high, high, low], axis=0))
    band = jnp.concatenate(bands, axis=1)

    rim_copy.wait()

    def along(c):
        along_copies[c].wait()
        high, low = split(rim_ref[c].reshape(count * rows, LANES))
        part = dot(jnp.concatenate([high, low, high], axis=1), band)
        part = part.reshape(count, rows, groups * width)
        extra = [part[:, :, width * q : width * (q + 1)] for q in range(groups)]
        return along_ref[c] + jnp.concatenate(extra, axis=1)

    inflow_planes(along, before, decay_ref, factor_ref, mean_ref, out_ref, planes_ref, prev_ref)


def previous_copy(previous, prev_ref, first, sem):
    width = prev_ref.shape[2]
    if width % LANES == 0:
        previous = previous.at[:, :, pl.ds(pl.multiple_of(first, LANES), width)]
    return pltpu.make_async_copy(previous, prev_ref, sem)


def inflow_planes(along, before, decay_ref, factor_ref, mean_ref, out_ref, planes_ref, prev_ref):
    comps, count, depth, width = planes_ref.shape
    zrow = lax.broadcasted_iota(jnp.int32, (depth, depth), 0)
    zcol = lax.broadcasted_iota(jnp.int32, (depth, depth), 1)
    zh, zl = split(weights(zrow - zcol))
    zband = jnp.concatenate([zh, zh, zl], axis=1)
    for c in range(comps):
        value = along(c)
        wide = jnp.concatenate([value[p] for p in range(count)], axis=1)
        yh, yl = split(wide)
        smooth = dot(zband, jnp.concatenate([yh, yl, yh], axis=0))
        if c == 0:
            before.wait()
        dec = column(decay_ref, c, width)
        scale = jnp.sqrt(1.0 - dec * dec)
        carried = prev_ref[c]
        for p in range(count):
            carried = dec * carried + scale * smooth[:, p * width : (p + 1) * width]
            planes_ref[c, p] = carried
    owners = out_ref.shape[0]
    slab = depth // owners

    def put(c, p, value):
        for d in range(owners):
            out_ref[d, c, p] = value[slab * d : slab * (d + 1)]

    mean = column(mean_ref, 0, width)
    factor = [column(factor_ref, i, width) for i in range(6)]
    for p in range(count):
        a, b, d = planes_ref[0, p], planes_ref[1, p], planes_ref[2, p]
        put(0, p, mean + factor[0] * a)
        put(1, p, factor[1] * a + factor[2] * b)
        put(2, p, factor[3] * a + factor[4] * b + factor[5] * d)


def sides(near, far, detour):
    line = lax.axis_index("grp")
    even = lax.rem(line, 2) == 0
    odd = (jnp.logical_not(even), near, far)
    if detour is None:
        return [(even, far, near), odd]
    return [(line == 2, detour, near), (jnp.logical_and(even, line != 2), far, near), odd]


def corners_kernel(*refs):
    near, far, *detour, _, up_ref, dn_ref, sem = refs
    slab = near.shape[2]

    def rows(left, right):
        copies = []
        for ref, z in ((up_ref, slab - 1), (dn_ref, 0)):
            for i, (face, x) in enumerate(((left, 1), (right, 0))):
                for c in range(3):
                    copies.append(
                        pltpu.make_async_copy(face.at[c, x, z], ref.at[c, i], sem.at[len(copies)])
                    )
        return copies

    for condition, left, right in sides(near, far, detour[0] if detour else None):

        @pl.when(condition)
        def _(left=left, right=right):
            run_copies(rows(left, right))


def inflow_faces_kernel(*refs):
    pieces = refs[:-3]
    dn, up, sem = refs[-3:]
    copies, first = [], 0
    for piece in pieces:
        count, slab = piece.shape[0], piece.shape[3]
        for j in range(2):
            for ref, z in ((dn, j), (up, slab - 2 + j)):
                copies.append(
                    pltpu.make_async_copy(
                        piece.at[:, :, :, z],
                        ref.at[pl.ds(first, count), :, j],
                        sem.at[len(copies)],
                    )
                )
        first += count

    @pl.when(lax.axis_index("grp") == 0)
    def _():
        run_copies(copies)


A = VISCOSITY * TIME_STEP
H = 0.5 * TIME_STEP
B = 1.0 - 6.0 * A
BLOCK = 512


def combine(scale, cs, xp, xn, zp, zn, yp, yn):
    a, h, b = A * scale, H * scale, B * scale
    cu, cw, cv = h * cs[0], h * cs[1], h * cs[2]
    out = []
    for i in range(3):
        total = xn[i] * (a - cu) + xp[i] * (a + cu)
        total = total + (zn[i] * (a - cw) + zp[i] * (a + cw))
        total = total + (yn[i] * (a - cv) + yp[i] * (a + cv))
        out.append(total + b * cs[i])
    return out


def spanwise(load, at, width, span):
    centre = load(at, width)
    wide = jnp.concatenate(
        [load((at - LANES) % span, LANES), centre, load((at + width) % span, LANES)], axis=1
    )
    total = width + 2 * LANES
    before = pltpu.roll(wide, 1, 1)[:, LANES : LANES + width]
    after = pltpu.roll(wide, total - 1, 1)[:, LANES : LANES + width]
    return centre, before, after


def main_block(scale, field, x, zb, za, zrow, at, width, span):
    top = lax.broadcasted_iota(jnp.int32, (SUB, width), 0)
    cs, xp, xn, zp, zn, yp, yn = [], [], [], [], [], [], []
    for c in range(3):
        centre, before, after = spanwise(
            lambda l, w, c=c: field[c, x, :, pl.ds(l, w)], at, width, span
        )
        cs.append(centre)
        yp.append(before)
        yn.append(after)
        xp.append(field[c, x - 1, :, pl.ds(at, width)])
        xn.append(field[c, x + 1, :, pl.ds(at, width)])
        low = jnp.broadcast_to(zb[c, pl.ds(zrow, 1), pl.ds(at, width)], (SUB, width))
        high = jnp.broadcast_to(za[c, pl.ds(zrow, 1), pl.ds(at, width)], (SUB, width))
        zp.append(jnp.where(top == 0, low, pltpu.roll(centre, 1, 0)))
        zn.append(jnp.where(top == SUB - 1, high, pltpu.roll(centre, SUB - 1, 0)))
    return combine(scale, cs, xp, xn, zp, zn, yp, yn)


def edge_rows(near, before, after, out, keep, begin, groups, span):
    def block(i, _):
        at = pl.multiple_of(i * BLOCK, BLOCK)
        left = pl.multiple_of(lax.rem(at + span - LANES, span), LANES)
        right = pl.multiple_of(lax.rem(at + BLOCK, span), LANES)
        for g in range(begin, groups):
            cs, xp, xn, zp, zn, yp, yn = [], [], [], [], [], [], []
            for c in range(3):
                r = SUB * (g + 1)
                centre = near[c, r : r + SUB, pl.ds(at, BLOCK)]
                wide = jnp.concatenate(
                    [
                        near[c, r : r + SUB, pl.ds(left, LANES)],
                        centre,
                        near[c, r : r + SUB, pl.ds(right, LANES)],
                    ],
                    axis=1,
                )
                total = BLOCK + 2 * LANES
                cs.append(centre)
                yp.append(pltpu.roll(wide, 1, 1)[:, LANES : LANES + BLOCK])
                yn.append(pltpu.roll(wide, total - 1, 1)[:, LANES : LANES + BLOCK])
                xp.append(near[c, r - 1 : r - 1 + SUB, pl.ds(at, BLOCK)])
                xn.append(near[c, r + 1 : r + 1 + SUB, pl.ds(at, BLOCK)])
                zp.append(before[c, SUB * g : SUB * (g + 1), pl.ds(at, BLOCK)])
                zn.append(after[c, SUB * g : SUB * (g + 1), pl.ds(at, BLOCK)])
            new = combine(1.0, cs, xp, xn, zp, zn, yp, yn)
            for c in range(3):
                out[c, SUB * (g + 1) : SUB * (g + 2), pl.ds(at, BLOCK)] = jnp.where(
                    keep, new[c], 0.0
                )
        return 0

    lax.fori_loop(0, span // BLOCK, block, 0)


def section_plane(x, start, sect, nb, na, span, keep=None):
    for at in range(0, span, BLOCK):
        new = main_block(1.0, start, x + 2, nb, na, SUB + x, at, BLOCK, span)
        for c in range(3):
            value = new[c] if keep is None else jnp.where(keep, new[c], 0.0)
            sect[c, x + 1, :, at : at + BLOCK] = value


def second_plane(x, start, sect, eb, ea, out, span):
    for at in range(0, span, BLOCK):
        new = main_block(0.5, sect, x + 1, eb, ea, SUB + x, at, BLOCK, span)
        for c in range(3):
            out[c, x, :, at : at + BLOCK] = new[c] + 0.5 * start[c, x + 2, :, at : at + BLOCK]


def rows_scratch(cells, span):
    shift = [
        pltpu.VMEM((3, cells + 2 * SUB, span), F32),
        pltpu.VMEM((3, cells + 2 * SUB, span), F32),
    ]
    side = [pltpu.VMEM((3, cells, span), F32)] * 4
    return shift + side + shift


def begin(copies, condition=None):
    if condition is not None:
        pl.when(condition)(lambda: begin(copies))
        return
    for copy in copies:
        copy.start()


def finish(copies, condition=None):
    if condition is not None:
        pl.when(condition)(lambda: finish(copies))
        return
    for copy in copies:
        copy.wait()


def run_copies(copies):
    for copy in copies:
        copy.start()
    for copy in copies:
        copy.wait()


def roles(rows, ranks):
    r, g = lax.axis_index("grp"), lax.axis_index("gx")
    return g > 0, g < ranks - 1, r > 0, r < rows - 1, r == 0


ROWS = ((2, 1, 0, SUB), (3, 0, 1, SUB), (2, 0, 2, 0), (0, 0, 3, 0), (1, 1, 4, 0), (3, 1, 5, 0))


def row_pieces(faces, first, *scratch):
    count = faces[0].shape[2]
    return [
        (faces[i].at[:, j], scratch[ref].at[:, pl.ds(at + first, count)])
        for i, j, ref, at in ROWS
    ]


def own_kernel(rows, ranks, vel, *refs):
    near, far, *detour = refs[:-25]
    (up_corners, dn_corners, dn_all, up_all, b_all, a_all, dn_hi, up_hi, b_hi, a_hi, out_hbm,
     start, sect, out, nb, na, b2, b0, a0, a2, eb, ea, corner, sem, out_sem) = refs[-25:]
    cells = vel.shape[1]
    low = cells - dn_hi.shape[2]
    span = vel.shape[3]
    has_before, has_after, has_left, has_right, is_first = roles(rows, ranks)
    first = jnp.where(is_first, low + 2, 0)
    is_other = jnp.logical_not(is_first)
    left_at, right_at = start.at[:, pl.ds(0, 2)], start.at[:, pl.ds(cells + 2, 2)]
    rows_first = row_pieces((dn_hi, up_hi, b_hi, a_hi), low, nb, na, b2, b0, a0, a2)
    rows_other = row_pieces((dn_all, up_all, b_all, a_all), 0, nb, na, b2, b0, a0, a2)
    ends = [(up_corners, corner.at[0]), (dn_corners, corner.at[1])]
    main = [(vel.at[:, pl.ds(low, cells - low)], start.at[:, pl.ds(2 + low, cells - low)])]
    rest = [(vel.at[:, pl.ds(0, low)], start.at[:, pl.ds(2, low)])]

    def copies(pieces, at):
        return [pltpu.make_async_copy(p, q, sem.at[at + i]) for i, (p, q) in enumerate(pieces)]

    begin(copies(rows_first, 0), is_first)
    begin(copies(rows_other, 0), is_other)
    begin(copies(ends, 6))
    begin(copies(main, 8))
    for condition, left, right in sides(near, far, detour[0] if detour else None):
        begin(copies([(right, right_at)], 9), condition)
        begin(copies([(left, left_at)], 10), jnp.logical_and(condition, is_other))
    begin(copies(rest, 11), is_other)
    finish(copies(rows_first, 0), is_first)
    finish(copies(rows_other, 0), is_other)
    finish(copies(ends, 6))

    @pl.when(jnp.logical_not(has_right))
    def _():
        for c in range(3):
            for i in range(2):
                corner[i, c, 1:2, :] = jnp.zeros((1, span), F32)

    for c in range(3):
        nb[c, SUB - 1 : SUB, :] = corner[0, c, 0:1, :]
        nb[c, SUB + cells : SUB + cells + 1, :] = corner[0, c, 1:2, :]
        na[c, SUB - 1 : SUB, :] = corner[1, c, 0:1, :]
        na[c, SUB + cells : SUB + cells + 1, :] = corner[1, c, 1:2, :]
    groups = cells // SUB

    @pl.when(jnp.logical_not(is_first))
    def _():
        edge_rows(nb, b2, b0, eb, has_before, 0, low // SUB, span)
        edge_rows(na, a0, a2, ea, has_after, 0, low // SUB, span)

    edge_rows(nb, b2, b0, eb, has_before, low // SUB, groups, span)
    edge_rows(na, a0, a2, ea, has_after, low // SUB, groups, span)
    finish(copies(main, 8))
    finish(copies([(near, right_at)], 9))
    finish(copies([(near, left_at)], 10), is_other)
    finish(copies(rest, 11), is_other)

    @pl.when(jnp.logical_not(has_right))
    def _():
        for c in range(3):
            start[c, cells + 2] = jnp.zeros((SUB, span), F32)

    def make(x, keep=None):
        section_plane(x, start, sect, nb, na, span, keep)

    def body(x, _):
        keep = jnp.logical_or(
            jnp.logical_and(x >= 0, x < cells),
            jnp.logical_or(jnp.logical_and(x < 0, has_left), jnp.logical_and(x >= cells, has_right)),
        )
        make(x, keep)

        @pl.when(x >= first + 1)
        def _():
            second_plane(x - 1, start, sect, eb, ea, out, span)
            pltpu.make_async_copy(out.at[:, x - 1], out_hbm.at[:, x - 1], out_sem.at[x - 1]).start()

        return 0

    lax.fori_loop(first - 1, cells + 1, body, 0)

    def drain(x, _):
        pltpu.make_async_copy(out.at[:, x], out_hbm.at[:, x], out_sem.at[x]).wait()
        return 0

    lax.fori_loop(first, cells, drain, 0)


def inflow_kernel(rows, ranks, groups_of, vel, *refs):
    many = sum(len(places) for places in groups_of)
    parts, refs = refs[:many], refs[many:]
    faces, refs = refs[: 4 * len(groups_of)], refs[4 * len(groups_of) :]
    dn_hi, up_hi, b_hi, a_hi, _, out_hbm = refs[:6]
    start, sect, out, nb, na, b2, b0, a0, a2, eb, ea, spread, sem, out_sem = refs[6:]
    cells = b2.shape[1]
    low = cells - dn_hi.shape[2]
    span = vel.shape[3]
    reach = out.shape[1]
    has_before, has_after, _, _, is_first = roles(rows, ranks)
    scratch = (nb, na, b2, b0, a0, a2)

    @pl.when(is_first)
    def _():
        edges = row_pieces((dn_hi, up_hi, b_hi, a_hi), low, *scratch)
        main = [(vel.at[:, pl.ds(low, 4)], start.at[:, pl.ds(low + 2, 4)])]
        lanes_of, at = [], 0
        for k, places in enumerate(groups_of):
            first = len(lanes_of)
            for piece, (source, part, parts_in) in zip(parts[at : at + len(places)], places):
                width = piece.shape[4]
                for i in range(piece.shape[0]):
                    lane = ((source + i) * parts_in + part) * width
                    main.append((piece.at[i], start.at[:, pl.ds(2, low), :, pl.ds(lane, width)]))
                    lanes_of.append(lane)
            at += len(places)
            for i in range(4):
                face = faces[4 * k + i]
                edges.append((face, spread.at[i, pl.ds(first, len(lanes_of) - first)]))
        edges = [pltpu.make_async_copy(p, q, sem.at[i]) for i, (p, q) in enumerate(edges)]
        main = [
            pltpu.make_async_copy(p, q, sem.at[len(edges) + i]) for i, (p, q) in enumerate(main)
        ]
        begin(edges)
        begin(main)
        zero = jnp.zeros((SUB, span), F32)
        for c in range(3):
            start[c, 1] = zero
            sect[c, 0] = zero
            for ref in (nb, na):
                ref[c, 0:SUB, :] = zero
                ref[c, SUB + cells :, :] = zero
        finish(edges)
        for n, lane in enumerate(lanes_of):
            for i, j, ref, first in ROWS:
                for c in range(3):
                    scratch[ref][c, first : first + low, lane : lane + LANES] = spread[i, n, c, j]
        groups = cells // SUB
        edge_rows(nb, b2, b0, eb, has_before, 0, groups, span)
        edge_rows(na, a0, a2, ea, has_after, 0, groups, span)
        finish(main)
        section_plane(0, start, sect, nb, na, span)

        def body(x, _):
            section_plane(x + 1, start, sect, nb, na, span)
            second_plane(x, start, sect, eb, ea, out, span)
            pltpu.make_async_copy(out.at[:, x], out_hbm.at[:, x], out_sem.at[x]).start()
            return 0

        lax.fori_loop(0, reach, body, 0)

        def drain(x, _):
            pltpu.make_async_copy(out.at[:, x], out_hbm.at[:, x], out_sem.at[x]).wait()
            return 0

        lax.fori_loop(0, reach, drain, 0)


def call(kernel, out_shape, out_specs, in_specs, scratch, estimate, alias=None):
    def run(*args):
        return pl.pallas_call(
            kernel,
            out_shape=out_shape,
            in_specs=in_specs,
            out_specs=out_specs,
            scratch_shapes=scratch,
            input_output_aliases=alias or {},
            compiler_params=params(),
            cost_estimate=estimate,
        )(*args)

    return run


def local(velocity, noise, previous, decay, stress_factor, mean_profile):
    rows = lax.axis_size("grp")
    ranks = lax.axis_size("gx")
    comps, count, depth, span_local = noise.shape
    cells, slab, span = velocity.shape[1:]
    width = span_local // PARTS
    low = count
    high = cells - low
    dma = pltpu.SemaphoreType.DMA

    def along_gx(array, step, lines, idlers=()):
        pairs = idle(idlers) + [
            (r * ranks + i, r * ranks + i + step)
            for r in lines
            for i in range(ranks)
            if 0 <= i + step < ranks
        ]
        return lax.ppermute(array, ("grp", "gx"), pairs)

    packed = jax.ShapeDtypeStruct((comps, count, depth * HALF // LANES, LANES), F32)
    face_hi = jax.ShapeDtypeStruct((3, 2, high, span), F32)
    xface = jax.ShapeDtypeStruct((3, 2, slab, span), F32)
    full = jax.ShapeDtypeStruct(velocity.shape, F32)
    rim_out, near_out, far_out = call(
        first_kernel,
        [packed, xface, xface],
        [VMEM] * 3,
        [ANY] * 2,
        [pltpu.VMEM((comps, count, depth, LANES), F32), dma((comps + 2,))],
        cost(0, noise.size),
    )(noise, velocity)

    def idle(lines):
        return [(r * ranks + i, r * ranks + (i ^ 1)) for r in lines for i in range(ranks)]

    def across(array, moves, idlers):
        pairs = [(a * ranks + i, b * ranks + i) for a, b in moves for i in range(ranks)]
        return lax.ppermute(array, ("grp", "gx"), pairs + idle(idlers))

    pairs = idle([r for r in range(rows) if r not in (1, 2)])
    for line, step in ((1, 1), (2, -1)):
        pairs += [(line * ranks + i, line * ranks + (i + step) % ranks) for i in range(ranks)]
    rim = lax.ppermute(rim_out, ("grp", "gx"), pairs)
    everyone = range(rows)
    evens = range(0, rows - 1, 2)
    odds = range(1, rows - 1, 2)
    lone = [0] + ([rows - 1] if rows % 2 == 0 else [])

    window = min(span_local, LANES * (-(-(width + 2 * HALF) // LANES) + 1))
    made_shape = jax.ShapeDtypeStruct((ranks, comps, count, depth // ranks, width), F32)

    windowed = pltpu.VMEM((comps, count, depth, window), F32)

    def make(kernel, inputs, specs, scratch):
        prev = previous
        if width % LANES:
            at = part_of(lax.axis_index("grp")) * width
            prev = lax.dynamic_slice_in_dim(previous, at, width, 2)
        return call(
            kernel,
            made_shape,
            VMEM,
            specs + [ANY, VMEM, VMEM, VMEM],
            [
                pltpu.VMEM((comps, count, depth, width), F32),
                pltpu.VMEM((comps, depth, width), F32),
            ]
            + scratch,
            cost(6 * noise.size * width, 4 * noise.size),
        )(*inputs, prev, decay, stress_factor, mean_profile[None])

    along = call(
        along_kernel,
        jax.ShapeDtypeStruct((comps, count, depth, width), F32),
        VMEM,
        [ANY],
        [windowed, dma((comps,))],
        cost(6 * noise.size * width, 4 * noise.size),
    )(noise)
    kernel_a = functools.partial(filter_kernel, span_local)
    made_a = make(
        kernel_a, [along, rim], [ANY] * 2,
        [
            pltpu.VMEM((comps, count, depth, width), F32),
            pltpu.VMEM(packed.shape, F32),
            dma((comps + 2,)),
        ],
    )
    got_a = lax.all_to_all(made_a, "gx", 0, 0, tiled=True)

    near = across(near_out, [p for i in evens for p in ((i, i + 1), (i + 1, i))], [])
    detour = []
    if rows == 4:
        far = across(far_out, [(1, 3), (2, 1)], [0])
        detour = [across(far, [(3, 2)], [0, 1])]
    else:
        far = across(far_out, [p for i in odds for p in ((i, i + 1), (i + 1, i))], lone)
    xfaces = [near, far] + detour
    face_all = jax.ShapeDtypeStruct((3, 2, cells, span), F32)
    dn_all, up_all, dn_hi, up_hi = call(
        zfaces_kernel, [face_all, face_all, face_hi, face_hi], [VMEM] * 4, [ANY] * 2,
        [dma((12,))], cost(0, velocity.size),
    )(velocity, made_a)
    others = range(1, rows)
    b_hi = along_gx(up_hi, 1, [0], others)
    a_hi = along_gx(dn_hi, -1, [0], others)

    half = ranks // 2
    first_half, last_half = got_a[:half], got_a[half:]
    side = lax.ppermute(last_half, "grp", [(3, 1)])
    hop_1 = lax.ppermute(got_a, "grp", [(1, 0)])
    hop_2 = lax.ppermute(got_a, "grp", [(2, 0)])
    hop_3 = lax.ppermute(first_half, "grp", [(3, 0)])

    b_all = along_gx(up_all, 1, others)
    a_all = along_gx(dn_all, -1, others)

    mark = call(
        mark_kernel, jax.ShapeDtypeStruct((SUB, LANES), F32), VMEM, [ANY], [], cost(0, 1024)
    )(made_a)
    pair = jax.ShapeDtypeStruct((3, 2, span), F32)
    up_corner, dn_corner = call(
        corners_kernel, [pair, pair], [VMEM] * 2, [ANY] * (len(xfaces) + 1), [dma((12,))],
        cost(0, 24 * span),
    )(*xfaces, mark)
    up_corners = along_gx(up_corner, 1, everyone)
    dn_corners = along_gx(dn_corner, -1, everyone)

    def fields(planes):
        return [
            pltpu.VMEM((3, planes + 4, slab, span), F32),
            pltpu.VMEM((3, planes + 2, slab, span), F32),
            pltpu.VMEM((3, planes, slab, span), F32),
        ]

    hop_4 = lax.ppermute(side, "grp", [(1, 0)])
    own = call(
        functools.partial(own_kernel, rows, ranks),
        full,
        ANY,
        [ANY] * (11 + len(xfaces)),
        fields(cells)
        + rows_scratch(cells, span)
        + [pltpu.VMEM((2, 3, 2, span), F32), dma((12,)), dma((cells,))],
        cost(50 * velocity.size, 8 * velocity.size),
    )(velocity, *xfaces, up_corners, dn_corners, dn_all, up_all, b_all, a_all, dn_hi, up_hi, b_hi,
      a_hi)

    parts = [[hop_1, got_a, hop_3, hop_4, hop_2]]
    groups_of = [
        [(0, 0, PARTS), (0, 1, PARTS), (0, 2, PARTS), (half, 2, PARTS), (0, 3, PARTS)]
    ]
    if width != LANES:
        joined = [hop_1, got_a, jnp.concatenate([hop_3, hop_4], axis=0), hop_2]
        joined = jnp.concatenate(joined, axis=4)
        parts = [[joined[..., at : at + LANES] for at in range(0, span_local, LANES)]]
        groups_of = [[(0, i, len(parts[0])) for i in range(len(parts[0]))]]
    faces = []
    for group in parts:
        number = sum(p.shape[0] for p in group)
        part_face = jax.ShapeDtypeStruct((number, 3, 2, low, LANES), F32)
        dn_in, up_in = call(
            inflow_faces_kernel,
            [part_face, part_face],
            [VMEM] * 2,
            [ANY] * len(group),
            [dma((4 * len(group),))],
            cost(0, 2 * noise.size),
        )(*group)
        b_in = along_gx(up_in, 1, [0])
        a_in = along_gx(dn_in, -1, [0])
        faces += [dn_in, up_in, b_in, a_in]
    parts = [p for group in parts for p in group]
    many = len(parts) + len(faces)
    number = sum(p.shape[0] for p in parts)

    reach = low + 2
    return call(
        functools.partial(inflow_kernel, rows, ranks, groups_of),
        full,
        ANY,
        [ANY] * (many + 6),
        fields(reach)
        + rows_scratch(low + high, span)
        + [
            pltpu.VMEM((4, number, 3, 2, low, LANES), F32),
            dma((number + 7 + len(faces),)),
            dma((reach,)),
        ],
        cost(30 * velocity.size, 5 * velocity.size),
        {many + 5: 0},
    )(velocity, *parts, *faces, dn_hi, up_hi, b_hi, a_hi, own)


def solution(mesh):
    placed = (
        P(None, "grp", "gx", None),
        P(None, None, None, "gx"),
        P(None, None, "gx"),
        P(),
        P(),
        P(),
    )

    return jax.shard_map(
        local, mesh=mesh, in_specs=placed, out_specs=P(None, "grp", "gx", None), check_vma=False
    )
```
